32 devices in a mesh: dp: 8 (over y, x, core), mp: 4 (over z).
Axes of the slice: x: 2, y: 2, z: 4, core: 2. Of those that a mesh axis runs over, the one named last changes fastest.
Arguments:
- latents: bfloat16 [8, 512, 1024], P('dp', 'mp'), may hold values from -6 to 6
- inputs: bfloat16 [8, 41472, 261], P('dp', 'mp'), may hold values from -6 to 6
- image_sizes: int32 [8], P('dp'), may hold values from 12800 to 41472, as said below
- latentgain: float32 [1024], replicated, may hold values from 0.25 to 1.75
- inputgain: float32 [261], replicated, may hold values from 0.25 to 1.75
- crossquery: bfloat16 [1024, 1024], replicated, may hold values from -0.375 to 0.375
- crosskey: bfloat16 [261, 1024], replicated, may hold values from -0.375 to 0.375
- crossvalue: bfloat16 [261, 1024], replicated, may hold values from -0.375 to 0.375
- crossoutput: bfloat16 [1024, 1024], replicated, may hold values from -3 to 3
- crossnorm: float32 [1024], replicated, may hold values from 0.25 to 1.75
- crossup: bfloat16 [1024, 1024], P(None, 'mp'), may hold values from -0.1875 to 0.1875
- crossdown: bfloat16 [1024, 1024], P('mp'), may hold values from -0.1875 to 0.1875
- selfnorm: float32 [1024], replicated, may hold values from 0.25 to 1.75
- selfquery: bfloat16 [1024, 1024], P(None, 'mp'), may hold values from -0.1875 to 0.1875
- selfkey: bfloat16 [1024, 1024], P(None, 'mp'), may hold values from -0.1875 to 0.1875
- selfvalue: bfloat16 [1024, 1024], P(None, 'mp'), may hold values from -0.1875 to 0.1875
- selfoutput: bfloat16 [1024, 1024], P('mp'), may hold values from -3 to 3
- mlpnorm: float32 [1024], replicated, may hold values from 0.25 to 1.75
- selfup: bfloat16 [1024, 1024], P(None, 'mp'), may hold values from -0.1875 to 0.1875
- selfdown: bfloat16 [1024, 1024], P('mp'), may hold values from -0.1875 to 0.1875
- cotangent: bfloat16 [8, 512, 1024], P('dp', 'mp'), may hold values from -6 to 6
Outputs:
- latents_out: bfloat16 [8, 512, 1024], P('dp', 'mp')
- latents_grad: float32 [8, 512, 1024], P('dp', 'mp')
- inputs_grad: float32 [8, 41472, 261], P('dp', 'mp')
- latentgain_grad: float32 [1024], replicated
- inputgain_grad: float32 [261], replicated
- crossquery_grad: float32 [1024, 1024], replicated
- crossing_key_gradient: float32 [261, 1024], replicated
- crossing_value_gradient: float32 [261, 1024], replicated
- crossoutput_grad: float32 [1024, 1024], replicated
- crossnorm_grad: float32 [1024], replicated
- crossup_grad: float32 [1024, 1024], P('dp', 'mp')
- crossdown_grad: float32 [1024, 1024], P('mp', 'dp')
- selfnorm_grad: float32 [1024], replicated
- latent_query_gradient: float32 [1024, 1024], P('dp', 'mp')
- latent_key_gradient: float32 [1024, 1024], P('dp', 'mp')
- latent_value_gradient: float32 [1024, 1024], P('dp', 'mp')
- latent_output_gradient: float32 [1024, 1024], P('mp', 'dp')
- mlpnorm_grad: float32 [1024], replicated
- selfup_grad: float32 [1024, 1024], P('dp', 'mp')
- selfdown_grad: float32 [1024, 1024], P('mp', 'dp')
The draws below stay inside these ranges and needn't reach their ends.
Inputs may be any that keep to these rules, and one draw needn't show every extreme that they name: Image i has its first image_sizes[i] input positions valid and the rest padding; each value is 12800, 25088 or 41472, and some image has 41472.
All inputs are finite; a program needn't handle non-finite values.
Results may differ from the reference program's by a relative error of at most 0.0165.
Values may be sent and summed in bfloat16 or wider, within the bound.
No kernel may reach another device: no remote copies, remote signals or barrier semaphores. Data moves between devices by JAX's collectives and lax.ppermute only.
A program may use at most 256 MiB of HBM per device.

```python
import jax
import jax.numpy as jnp
from jax import lax

D = 1024
LAT = 512
IN_CH = 261
HEADS = 8
FF = 1024
SQ = 512
INPUTS = 41472
IMAGES = 8


def draw_image_sizes(key, part):
    classes = jax.random.randint(key, (IMAGES,), 0, 3)
    chosen = jax.random.randint(jax.random.fold_in(key, 7), (), 0, IMAGES)
    classes = jnp.where(jnp.arange(IMAGES) == chosen, 2, classes)
    factor = jnp.where(classes == 0, 25, jnp.where(classes == 1, 49, 81))
    return (factor * SQ).astype(jnp.int32)


def shard_levels(own_key, dims, pieces, smallest, top_value):
    def one(position, blocks):
        draws = jax.random.uniform(jax.random.fold_in(jax.random.fold_in(own_key, 6), position), (blocks,), jnp.float32, smallest / len(pieces), top_value / len(pieces))
        return jnp.repeat(jnp.exp(draws), dims[position] // blocks).reshape((-1,) + (1,) * (len(dims) - position - 1))

    level = one(*pieces[0])
    for cut in pieces[1:]:
        level = level * one(*cut)
    return level


def normal_values(rng, extent, scale, bound, split=(), kind=jnp.bfloat16):
    gain = shard_levels(rng, extent, split, -0.22, 0.18) if split else 1.0
    entries = jax.random.normal(rng, extent, jnp.float32) * scale * gain
    return jnp.minimum(jnp.maximum(entries, -bound), bound).astype(kind)


def setup_inputs(seed: int = 0) -> dict:
    arg_keys = jax.random.split(jax.random.key(seed), 22)
    return {
        "latents": normal_values(arg_keys[0], (IMAGES, LAT, D), 1.0, 6.0, ((0, 8), (1, 4))),
        "inputs": normal_values(arg_keys[1], (IMAGES, INPUTS, IN_CH), 1.0, 6.0, ((0, 8), (1, 4))),
        "image_sizes": draw_image_sizes(jax.random.fold_in(arg_keys[21], 71), 0),
        "latentgain": jnp.clip(1.0 + 0.15 * jax.random.normal(arg_keys[3], (D,), jnp.float32), 0.25, 1.75),
        "inputgain": jnp.clip(1.0 + 0.15 * jax.random.normal(arg_keys[4], (IN_CH,), jnp.float32), 0.25, 1.75),
        "crossquery": normal_values(arg_keys[5], (D, D), (D // 4) ** -0.5, 0.375),
        "crosskey": normal_values(arg_keys[6], (IN_CH, D), IN_CH ** -0.5, 0.375),
        "crossvalue": normal_values(arg_keys[7], (IN_CH, D), IN_CH ** -0.5, 0.375),
        "crossoutput": normal_values(arg_keys[8], (D, D), 4 ** -0.5, 3.0),
        "crossnorm": jnp.clip(1.0 + 0.15 * jax.random.normal(arg_keys[9], (D,), jnp.float32), 0.25, 1.75),
        "crossup": normal_values(arg_keys[10], (D, FF), D ** -0.5, 0.1875, ((1, 4),)),
        "crossdown": normal_values(arg_keys[11], (FF, D), FF ** -0.5, 0.1875, ((0, 4),)),
        "selfnorm": jnp.clip(1.0 + 0.15 * jax.random.normal(arg_keys[12], (D,), jnp.float32), 0.25, 1.75),
        "selfquery": normal_values(arg_keys[13], (D, D), D ** -0.5, 0.1875, ((1, 4),)),
        "selfkey": normal_values(arg_keys[14], (D, D), D ** -0.5, 0.1875, ((1, 4),)),
        "selfvalue": normal_values(arg_keys[15], (D, D), D ** -0.5, 0.1875, ((1, 4),)),
        "selfoutput": normal_values(arg_keys[16], (D, D), 4 ** -0.5, 3.0, ((0, 4),)),
        "mlpnorm": jnp.clip(1.0 + 0.15 * jax.random.normal(arg_keys[17], (D,), jnp.float32), 0.25, 1.75),
        "selfup": normal_values(arg_keys[18], (D, FF), D ** -0.5, 0.1875, ((1, 4),)),
        "selfdown": normal_values(arg_keys[19], (FF, D), FF ** -0.5, 0.1875, ((0, 4),)),
        "cotangent": normal_values(arg_keys[20], (IMAGES, LAT, D), 1.0, 6.0, ((0, 8), (1, 4))),
    }


@jax.custom_vjp
def low(v):
    return lax.optimization_barrier(v.astype(jnp.bfloat16)).astype(jnp.float32)

@jax.custom_vjp
def low_back(v):
    return v

def low_keep(v):
    return (low(v), None)

def low_pass(kept, grad):
    return (grad,)

def back_keep(v):
    return (v, None)

def back_low(kept, grad):
    return (low(grad),)
low.defvjp(low_keep, low_pass)
low_back.defvjp(back_keep, back_low)
HIGH = lax.Precision.HIGHEST
EPSILON = 1e-05
MASKED = -1e+30

def layer_norm(values, layernorm_multiplier):
    centred = values - lax.optimization_barrier(jnp.mean(values, axis=-1, keepdims=True))
    spread = lax.optimization_barrier(jnp.mean(centred * centred, axis=-1, keepdims=True))
    return centred * lax.rsqrt(spread + EPSILON) * layernorm_multiplier

def matmul(left_side, right_side):
    return jnp.dot(left_side, right_side, precision=HIGH, preferred_element_type=jnp.float32)

def feed_forward(residual, layernorm_multiplier, expanding_matrix, down_projection_weight):
    normed = low(layer_norm(residual, layernorm_multiplier))
    hidden_units = low_back(matmul(normed, expanding_matrix))
    activated_units = low(jax.nn.gelu(hidden_units, approximate=True))
    return residual + low_back(matmul(activated_units, down_projection_weight))

def cross_block(latent_rows, input_rows, unpadded_length, latentgain, inputgain, crossquery, crosskey, crossvalue, crossoutput, crossnorm, crossup, crossdown):
    normed_latent = low(layer_norm(latent_rows, latentgain))
    queries = low_back(low(matmul(normed_latent, crossquery)))
    normalized_input = low(layer_norm(input_rows, inputgain))
    key_rows = low_back(low(matmul(normalized_input, crosskey)))
    value_rows = low_back(low(matmul(normalized_input, crossvalue)))
    valid_keys = (jnp.arange(INPUTS, dtype=jnp.int32) < unpadded_length)[None, :]
    scores = low_back(matmul(queries, key_rows.T)) * D ** (-0.5)
    scores = jnp.where(valid_keys, scores, MASKED)
    highest = lax.optimization_barrier(jnp.max(scores, axis=-1, keepdims=True))
    summed = lax.optimization_barrier(jnp.sum(jnp.where(valid_keys, jnp.exp(scores - highest), 0.0), axis=-1, keepdims=True))
    log_total = highest + jnp.log(summed)
    cross_probs = jnp.where(valid_keys, jnp.exp(scores - log_total), 0.0)
    mixed = low_back(low(matmul(low(cross_probs), value_rows)))
    first_resid = latent_rows + low_back(matmul(mixed, crossoutput))
    return feed_forward(first_resid, crossnorm, crossup, crossdown)

def self_block(residual, selfnorm, selfquery, selfkey, selfvalue, selfoutput, mlpnorm, selfup, selfdown):
    head_size = D // HEADS
    normed = low(layer_norm(residual, selfnorm))
    queries = low_back(low(matmul(normed, selfquery))).reshape(LAT, HEADS, head_size)
    keys_all = low_back(low(matmul(normed, selfkey))).reshape(LAT, HEADS, head_size)
    values_all = low_back(low(matmul(normed, selfvalue))).reshape(LAT, HEADS, head_size)
    unscaled_scores = jnp.einsum('qhe,khe->hqk', queries, keys_all, precision=HIGH)
    scores = low_back(unscaled_scores) * head_size ** (-0.5)
    highest = lax.optimization_barrier(jnp.max(scores, axis=-1, keepdims=True))
    self_log = highest + jnp.log(lax.optimization_barrier(jnp.sum(jnp.exp(scores - highest), axis=-1, keepdims=True)))
    self_probs = jnp.exp(scores - self_log)
    attended = jnp.einsum('hqk,khe->qhe', low(self_probs), values_all, precision=HIGH).reshape(LAT, D)
    attended = low_back(low(attended))
    third_residual = residual + low_back(matmul(attended, selfoutput))
    return feed_forward(third_residual, mlpnorm, selfup, selfdown)

def reference(latents, inputs, image_sizes, latentgain, inputgain, crossquery, crosskey, crossvalue, crossoutput, crossnorm, crossup, crossdown, selfnorm, selfquery, selfkey, selfvalue, selfoutput, mlpnorm, selfup, selfdown, cotangent):
    floats = tuple((array.astype(jnp.float32) for array in (latents, inputs, latentgain, inputgain, crossquery, crosskey, crossvalue, crossoutput, crossnorm, crossup, crossdown, selfnorm, selfquery, selfkey, selfvalue, selfoutput, mlpnorm, selfup, selfdown)))

    def forward(latent_all, input_all, gain_latent, gain_input, cross_q, cross_k, cross_v, cross_o, cross_n, cross_u, cross_d, self_n, self_q, self_k, self_v, self_o, mlp_n, self_u, self_d):

        def one_image(item):
            latent_rows, input_rows, unpadded_length = item
            middle = cross_block(latent_rows, input_rows, unpadded_length, gain_latent, gain_input, cross_q, cross_k, cross_v, cross_o, cross_n, cross_u, cross_d)
            return self_block(middle, self_n, self_q, self_k, self_v, self_o, mlp_n, self_u, self_d)
        return lax.map(jax.checkpoint(one_image), (latent_all, input_all, image_sizes))
    result, pullback = jax.vjp(forward, *floats)
    grads = pullback(cotangent.astype(jnp.float32))
    return (result.astype(jnp.bfloat16), grads[0], grads[1], grads[2], grads[3], grads[4], grads[5], grads[6], grads[7], grads[8], grads[9], grads[10], grads[11], grads[12], grads[13], grads[14], grads[15], grads[16], grads[17], grads[18])
```

```python
import functools

import jax
import jax.numpy as jnp
from jax import lax
from jax.experimental import pallas as pl
from jax.experimental.pallas import tpu as pltpu
from jax.sharding import PartitionSpec as P

HEADS = 8
EPSILON = 1e-05
MASKED = -1e30
FLOOR = -1e25
TILE = 1152
VMEM_LIMIT = 60 * 1024 * 1024
BF16 = jnp.bfloat16
F32 = jnp.float32
NN = (((1,), (0,)), ((), ()))
NT = (((1,), (1,)), ((), ()))
TN = (((0,), (0,)), ((), ()))


def dot(left, right, dims):
    return lax.dot_general(left, right, dims, preferred_element_type=F32)


def padded_rows(channels):
    return -(-(channels + 3) // 16) * 16


def normalized(raw_ref, channels, head_rows):
    top = raw_ref[:head_rows, :].astype(F32)
    rest = raw_ref[head_rows:, :].astype(F32)
    keep = lax.broadcasted_iota(jnp.int32, rest.shape, 0) < (channels - head_rows)
    rest = jnp.where(keep, rest, 0.0)
    mean = (jnp.sum(top, 0, keepdims=True) + jnp.sum(rest, 0, keepdims=True)) * (1.0 / channels)
    top = top - mean
    rest = jnp.where(keep, rest - mean, 0.0)
    square = jnp.sum(top * top, 0, keepdims=True) + jnp.sum(rest * rest, 0, keepdims=True)
    scale = lax.rsqrt(square * (1.0 / channels) + EPSILON)
    return top * scale, rest * scale, scale, keep


def prepare_kernel(limit_ref, raw_ref, gain_ref, out_ref, *, channels, head_rows):
    top, rest, _, keep = normalized(raw_ref, channels, head_rows)
    out_ref[:head_rows, :] = (top * gain_ref[:head_rows, :]).astype(BF16)
    lane = pl.program_id(0) * TILE + lax.broadcasted_iota(jnp.int32, rest.shape, 1)
    row = lax.broadcasted_iota(jnp.int32, rest.shape, 0) + head_rows
    invalid = jnp.where(lane < limit_ref[0], 0.0, 1.0)
    ones = (row == channels) | (row == channels + 2)
    extra = jnp.where(row == channels + 1, invalid, jnp.where(ones, 1.0, 0.0))
    out_ref[head_rows:, :] = jnp.where(keep, rest * gain_ref[head_rows:, :], extra).astype(BF16)


def prepare(limit, raw, gain_column):
    channels, count = raw.shape
    rows = padded_rows(channels)
    tiles = pl.cdiv(count, TILE)
    return pl.pallas_call(
        functools.partial(prepare_kernel, channels=channels, head_rows=rows - 16),
        grid_spec=pltpu.PrefetchScalarGridSpec(
            num_scalar_prefetch=1,
            grid=(tiles,),
            in_specs=[
                pl.BlockSpec((rows, TILE), lambda i, _: (0, i)),
                pl.BlockSpec((rows, 1), lambda i, _: (0, 0)),
            ],
            out_specs=pl.BlockSpec((rows, TILE), lambda i, _: (0, i)),
        ),
        out_shape=jax.ShapeDtypeStruct((rows, tiles * TILE), BF16),
        compiler_params=pltpu.CompilerParams(vmem_limit_bytes=VMEM_LIMIT),
        name="prepare",
    )(limit, raw, gain_column)


def forward_kernel(x_ref, a_ref, p_ref, y_ref, top_ref, running):
    @pl.when(pl.program_id(0) == 0)
    def _():
        running[...] = jnp.full_like(running, FLOOR)
        y_ref[...] = jnp.zeros_like(y_ref)

    x = x_ref[...]
    scores = dot(x, a_ref[...], TN)
    old = running[0:1, :]
    new = jnp.maximum(old, jnp.max(scores, 0, keepdims=True))
    probs = jnp.exp(scores - new).astype(BF16)
    p_ref[...] = probs
    y_ref[...] = y_ref[...] * jnp.exp(old - new) + dot(x, probs, NN)
    running[0:1, :] = new
    top_ref[0] = new


def cross_forward(x, a):
    rows, count = x.shape
    queries = a.shape[1]
    tiles = count // TILE
    return pl.pallas_call(
        forward_kernel,
        grid=(tiles,),
        in_specs=[
            pl.BlockSpec((rows, TILE), lambda i: (0, i)),
            pl.BlockSpec((rows, queries), lambda i: (0, 0)),
        ],
        out_specs=[
            pl.BlockSpec((TILE, queries), lambda i: (i, 0)),
            pl.BlockSpec((rows, queries), lambda i: (0, 0)),
            pl.BlockSpec((1, 1, queries), lambda i: (i, 0, 0)),
        ],
        out_shape=[
            jax.ShapeDtypeStruct((count, queries), BF16),
            jax.ShapeDtypeStruct((rows, queries), F32),
            jax.ShapeDtypeStruct((tiles, 1, queries), F32),
        ],
        scratch_shapes=[pltpu.VMEM((8, queries), F32)],
        compiler_params=pltpu.CompilerParams(vmem_limit_bytes=VMEM_LIMIT),
        name="cross_forward",
    )(x, a)


def lane_sums(values):
    total = values[:, :128]
    for k in range(1, values.shape[1] // 128):
        total = total + values[:, 128 * k : 128 * (k + 1)]
    return total


def backward_kernel(
    limit_ref,
    raw_ref,
    x_ref,
    p_ref,
    factor_ref,
    a_ref,
    b_ref,
    gain_ref,
    out_ref,
    z_ref,
    gain_grad_ref,
    *,
    channels,
    head_rows,
    guard,
):
    @pl.when(pl.program_id(0) == 0)
    def _():
        z_ref[...] = jnp.zeros_like(z_ref)
        gain_grad_ref[...] = jnp.zeros_like(gain_grad_ref)

    x = x_ref[...]
    slope = dot(x, b_ref[...], TN)
    probs = p_ref[...].astype(F32) * factor_ref[0]
    score_grad = (probs * slope).astype(BF16)
    probs = probs.astype(BF16)
    z_ref[...] += dot(x, score_grad, NN)
    grad = dot(a_ref[...], score_grad, NT) + dot(b_ref[...], probs, NT)
    top, rest, scale, keep = normalized(raw_ref, channels, head_rows)
    grad_top = grad[:head_rows]
    grad_rest = jnp.where(keep, grad[head_rows:], 0.0)
    if guard:
        lane = pl.program_id(0) * TILE + lax.broadcasted_iota(jnp.int32, (1, TILE), 1)
        inside = lane < limit_ref[0]
        grad_top = jnp.where(inside, grad_top, 0.0)
        grad_rest = jnp.where(inside, grad_rest, 0.0)
        top = jnp.where(inside, top, 0.0)
        rest = jnp.where(inside, rest, 0.0)
        scale = jnp.where(inside, scale, 0.0)
    gain_grad_ref[:head_rows, :] += lane_sums(grad_top * top)
    gain_grad_ref[head_rows:, :] += lane_sums(grad_rest * rest)
    grad_top = grad_top * gain_ref[:head_rows, :]
    grad_rest = grad_rest * gain_ref[head_rows:, :]
    mean = jnp.sum(grad_top, 0, keepdims=True) + jnp.sum(grad_rest, 0, keepdims=True)
    along = jnp.sum(grad_top * top, 0, keepdims=True) + jnp.sum(grad_rest * rest, 0, keepdims=True)
    mean = mean * (1.0 / channels)
    along = along * (1.0 / channels)
    out_ref[:head_rows, 0, :] = (grad_top - mean - top * along) * scale
    out_rest = (grad_rest - mean - rest * along) * scale
    out_ref[head_rows:, 0, :] = out_rest[: channels - head_rows]


def cross_backward(limit, raw, x, probs, factor, a, b, gain_column):
    channels, real = raw.shape
    rows, count = x.shape
    queries = a.shape[1]
    tiles = count // TILE
    return pl.pallas_call(
        functools.partial(
            backward_kernel, channels=channels, head_rows=rows - 16, guard=count != real
        ),
        grid_spec=pltpu.PrefetchScalarGridSpec(
            num_scalar_prefetch=1,
            grid=(tiles,),
            in_specs=[
                pl.BlockSpec((rows, TILE), lambda i, _: (0, i)),
                pl.BlockSpec((rows, TILE), lambda i, _: (0, i)),
                pl.BlockSpec((TILE, queries), lambda i, _: (i, 0)),
                pl.BlockSpec((1, 1, queries), lambda i, _: (i, 0, 0)),
                pl.BlockSpec((rows, queries), lambda i, _: (0, 0)),
                pl.BlockSpec((rows, queries), lambda i, _: (0, 0)),
                pl.BlockSpec((rows, 1), lambda i, _: (0, 0)),
            ],
            out_specs=[
                pl.BlockSpec((channels, 1, TILE), lambda i, _: (0, 0, i)),
                pl.BlockSpec((rows, queries), lambda i, _: (0, 0)),
                pl.BlockSpec((rows, 128), lambda i, _: (0, 0)),
            ],
        ),
        out_shape=[
            jax.ShapeDtypeStruct((channels, 1, real), F32),
            jax.ShapeDtypeStruct((rows, queries), F32),
            jax.ShapeDtypeStruct((rows, 128), F32),
        ],
        compiler_params=pltpu.CompilerParams(vmem_limit_bytes=VMEM_LIMIT),
        name="cross_backward",
    )(limit, raw, x, probs, factor, a, b, gain_column)


def shifted(block, distance):
    size = lax.axis_size("mp")
    return lax.ppermute(block, "mp", [(i, (i + distance) % size) for i in range(size)])


def gathered(block):
    size = lax.axis_size("mp")
    return [block] + [shifted(block, d) for d in range(1, size)]


def exchanged(blocks):
    return [blocks[0]] + [shifted(blocks[d], -d) for d in range(1, len(blocks))]


def summed_rows(partial):
    size = lax.axis_size("mp")
    blocks = jnp.split(partial, size, axis=0)
    sent = [blocks[0]] + [block.astype(BF16) for block in blocks[1:]]
    total = sent[0]
    for block in exchanged(sent)[1:]:
        total = total + block.astype(F32)
    return total


def reduced_everywhere(values, held, later):
    data, size = lax.axis_size("dp"), lax.axis_size("mp")
    index = lax.axis_index("dp")
    bits = [1 << k for k in range(data.bit_length() - 1)]
    for bit in bits:
        low, high = jnp.split(values, 2, axis=1)
        upper = (index & bit) != 0
        mine = jnp.where(upper, high, low)
        other = jnp.where(upper, low, high).astype(BF16)
        swap = [(i, i ^ bit) for i in range(data)]
        values = mine + lax.ppermute(other, "dp", swap).astype(F32)
        if bit == bits[0]:
            values, held = lax.optimization_barrier((values, held))
    rows, columns = values.shape
    chunks = values.reshape(size, rows // size, columns)
    place = lax.axis_index("mp")

    def chunk(k):
        return lax.dynamic_index_in_dim(chunks, (place + k) % size, 0, keepdims=False)

    total = chunk(0)
    for d in range(1, size):
        total = total + shifted(chunk(d).astype(BF16), d).astype(F32)
    own = total.astype(BF16)
    full = jnp.zeros((size,) + own.shape, BF16)
    for d, block in enumerate(gathered(own)):
        full = lax.dynamic_update_index_in_dim(full, block, (place - d) % size, 0)
    full = full.reshape(rows, columns)
    full, later = lax.optimization_barrier((full, later))
    for bit in reversed(bits):
        swap = [(i, i ^ bit) for i in range(data)]
        other = lax.ppermute(full, "dp", swap)
        upper = (index & bit) != 0
        full = jnp.where(
            upper, jnp.concatenate([other, full], 1), jnp.concatenate([full, other], 1)
        )
    return full, held, later


def standardized(values):
    centred = values - jnp.mean(values, axis=-1, keepdims=True)
    spread = jnp.mean(centred * centred, axis=-1, keepdims=True)
    scale = lax.rsqrt(spread + EPSILON)
    return centred * scale, scale


def norm_backward(hat, scale, gain, upstream):
    weighted = upstream * gain
    mean = jnp.mean(weighted, axis=-1, keepdims=True)
    along = jnp.mean(weighted * hat, axis=-1, keepdims=True)
    return (weighted - mean - hat * along) * scale, jnp.sum(upstream * hat, axis=0)


def gelu_tanh(values):
    return jax.nn.gelu(values, approximate=True)


def gelu_backward(values, upstream):
    return jax.vjp(gelu_tanh, values)[1](upstream)[0]


def whole_weights(up, down):
    data = lax.axis_size("dp")
    index = lax.axis_index("dp")
    pair = jnp.stack([up.T, down])
    part = pair.shape[1] // data
    piece = lax.dynamic_slice_in_dim(pair, index * part, part, 1)
    full = lax.all_gather(piece, ("mp", "dp"), axis=1, tiled=True)
    return full[0], full[1]


def mlp_forward(residual, gain, up, down):
    hat, scale = standardized(residual)
    normed = (hat * gain).astype(BF16)
    hidden = dot(normed, up, NT)
    active = gelu_tanh(hidden).astype(BF16)
    return residual + dot(active, down, NN), (hat, scale, normed, hidden, active)


def mlp_backward(upstream, gain, up, down, stored):
    hat, scale, normed, hidden, active = stored
    low = upstream.astype(BF16)
    active_grad = dot(low, down, NT)
    hidden_grad = gelu_backward(hidden, active_grad).astype(BF16)
    normed_grad = dot(hidden_grad, up, NN)
    input_grad, gain_grad = norm_backward(hat, scale, gain, normed_grad)
    return upstream + input_grad, gain_grad, (normed, hidden_grad, low, active)


def pair_gradients(operands):
    normed, hidden_grad, low, active = operands
    size = lax.axis_size("mp")
    grads = (dot(normed, hidden_grad, TN), dot(low, active, TN))
    pieces = [jnp.split(grad.astype(BF16), size, axis=1) for grad in grads]
    return jnp.concatenate([piece[k] for k in range(size) for piece in pieces], axis=1)


def summed_over_images(stacked):
    return lax.psum_scatter(stacked, "dp", scatter_dimension=0, tiled=True)


def scattered_pair(mine):
    size = lax.axis_size("mp")
    part = mine.shape[1] // size
    place = lax.axis_index("mp")

    def chunk(k):
        return lax.dynamic_slice_in_dim(mine, (place + k) % size * part, part, 1)

    total = chunk(0).astype(F32)
    for d in range(1, size):
        total = total + shifted(chunk(d), d).astype(F32)
    first, second = jnp.split(total, 2, axis=1)
    return first, second.T


def shards(
    latents,
    inputs,
    image_sizes,
    latentgain,
    inputgain,
    crossquery,
    crosskey,
    crossvalue,
    crossoutput,
    crossnorm,
    crossup,
    crossdown,
    selfnorm,
    selfquery,
    selfkey,
    selfvalue,
    selfoutput,
    mlpnorm,
    selfup,
    selfdown,
    cotangent,
):
    width = latents.shape[-1]
    channels = inputs.shape[-1]
    count = inputs.shape[1]
    head_size = width // HEADS
    rows = padded_rows(channels)
    group = lax.axis_size("mp")
    cross_scale = width**-0.5
    self_scale = head_size**-0.5

    cross_up, cross_down = whole_weights(crossup, crossdown)
    self_up, self_down = whole_weights(selfup, selfdown)

    latent_float = latents[0].astype(F32)
    padding = ((0, rows - channels), (0, 0))
    key_weight = jnp.pad(crosskey, padding)
    value_weight = jnp.pad(crossvalue, padding)
    key_map = dot(key_weight, crossquery, NT).astype(BF16)
    value_map = dot(value_weight, crossoutput, NN).astype(BF16)

    latent_hat, latent_scale = standardized(latent_float)
    normed_latent = (latent_hat * latentgain).astype(BF16)
    row_index = lax.broadcasted_iota(jnp.int32, (rows, 1), 0)
    score_map = dot(key_map, normed_latent, NT) * cross_scale
    score_map = jnp.where(row_index == channels + 1, MASKED, score_map).astype(BF16)
    score_maps = jnp.concatenate(gathered(score_map), axis=1)
    hat_rows = jnp.concatenate(gathered(latent_hat.astype(BF16)), axis=0)

    limit = jnp.clip(image_sizes - lax.axis_index("mp") * count, 0, count)
    extent = jnp.full((1,), count, jnp.int32)
    raw = inputs[0].T
    gain_column = jnp.pad(inputgain[:, None], padding)
    x = prepare(limit, raw, gain_column)
    probs, partial, tops = cross_forward(x, score_maps)

    partial = jnp.where(row_index == channels + 1, tops[-1], partial)
    parts = exchanged(jnp.split(partial, group, axis=1))
    part_tops = [part[channels + 1 : channels + 2] for part in parts]
    top = functools.reduce(jnp.maximum, part_tops)
    mixed = sum(part * jnp.exp(part_top - top) for part, part_top in zip(parts, part_tops))
    total = mixed[channels : channels + 1]
    log_total = top + jnp.log(total)
    mixed = jnp.where(row_index < channels, mixed / total, 0.0)
    log_all = jnp.concatenate(gathered(log_total), axis=1)
    factor = jnp.exp(tops - log_all[None])
    mixed_low = mixed.astype(BF16)

    first_resid = latent_float + dot(mixed_low, value_map, TN)
    second_resid, cross_stored = mlp_forward(first_resid, crossnorm, cross_up, cross_down)

    self_hat, self_norm_scale = standardized(second_resid)
    normed_self = (self_hat * selfnorm).astype(BF16)
    self_rows = jnp.concatenate(gathered(normed_self), axis=0)
    tokens = self_rows.shape[0]
    projections = jnp.concatenate([selfquery, selfkey, selfvalue], axis=1)
    block = selfquery.shape[1]
    projected = dot(self_rows, projections, NN).astype(BF16)

    def heads_of(flat):
        return flat.reshape(tokens, -1, head_size)

    queries, keys, values = (
        heads_of(projected[:, k * block : (k + 1) * block]) for k in range(3)
    )

    def product(pattern, left, right):
        return jnp.einsum(pattern, left, right, preferred_element_type=F32)

    scores = product("qhe,khe->hqk", queries, keys) * self_scale
    self_top = jnp.max(scores, axis=-1, keepdims=True)
    powers = jnp.exp(scores - self_top)
    self_probs = powers / jnp.sum(powers, axis=-1, keepdims=True)
    self_low = self_probs.astype(BF16)
    attended = product("hqk,khe->qhe", self_low, values).reshape(tokens, -1).astype(BF16)
    third_resid = second_resid + summed_rows(dot(attended, selfoutput, NN))
    final_resid, self_stored = mlp_forward(third_resid, mlpnorm, self_up, self_down)
    latents_out = final_resid.astype(BF16)

    upstream = cotangent[0].astype(F32)
    third_grad, mlpnorm_grad, self_pair = mlp_backward(
        upstream, mlpnorm, self_up, self_down, self_stored
    )
    third_low, self_pair = lax.optimization_barrier((third_grad.astype(BF16), self_pair))
    third_rows = jnp.concatenate(gathered(third_low), axis=0)
    third_rows, self_pair = lax.optimization_barrier((third_rows, pair_gradients(self_pair)))
    self_pair = summed_over_images(self_pair)
    attended_grad = heads_of(dot(third_rows, selfoutput, NT).astype(BF16))
    self_probs_grad = product("qhe,khe->hqk", attended_grad, values)
    self_row = jnp.sum(self_probs * self_probs_grad, axis=-1, keepdims=True)
    scores_grad = (self_probs * (self_probs_grad - self_row) * self_scale).astype(BF16)
    values_grad = product("hqk,qhe->khe", self_low, attended_grad)
    queries_grad = product("hqk,khe->qhe", scores_grad, keys)
    keys_grad = product("hqk,qhe->khe", scores_grad, queries)
    projected_grad = jnp.concatenate(
        [grad.reshape(tokens, -1).astype(BF16) for grad in (queries_grad, keys_grad, values_grad)],
        axis=1,
    )
    normed_part = dot(projected_grad, projections, NT)
    normed_part, sources = lax.optimization_barrier(
        (normed_part, (self_rows, projected_grad, third_rows, attended))
    )
    normed_self_grad = summed_rows(normed_part)
    attention_grads = jnp.concatenate(
        [dot(sources[0], sources[1], TN), dot(sources[2], sources[3], TN)], axis=1
    ).astype(BF16)
    normed_self_grad, attention_grads = lax.optimization_barrier(
        (normed_self_grad, attention_grads)
    )
    attention_grads = summed_over_images(attention_grads).astype(F32)
    query_grad, key_grad, value_grad, output_grad = jnp.split(attention_grads, 4, axis=1)

    second_input_grad, selfnorm_grad = norm_backward(
        self_hat, self_norm_scale, selfnorm, normed_self_grad
    )
    second_grad = third_grad + second_input_grad
    first_grad, crossnorm_grad, cross_pair = mlp_backward(
        second_grad, crossnorm, cross_up, cross_down, cross_stored
    )
    first_low = first_grad.astype(BF16)
    slope_map = dot(value_map, first_low, NT).astype(BF16)
    offset = -jnp.sum(slope_map.astype(F32) * mixed, axis=0, keepdims=True)
    offset_high = offset.astype(BF16)
    offset_low = (offset - offset_high.astype(F32)).astype(BF16)
    slope_map = jnp.where(row_index == channels, offset_high, slope_map)
    slope_map = jnp.where(row_index == channels + 2, offset_low, slope_map)
    slope_map, cross_pair = lax.optimization_barrier((slope_map, cross_pair))
    slope_maps = jnp.concatenate(gathered(slope_map), axis=1)
    slope_maps, cross_pair, self_pair = lax.optimization_barrier(
        (slope_maps, pair_gradients(cross_pair), self_pair)
    )
    cross_pair = summed_over_images(cross_pair)
    selfup_grad, selfdown_grad = scattered_pair(self_pair)
    inputs_grad, partial_z, partial_gain = cross_backward(
        extent, raw, x, probs, factor, score_maps, slope_maps, gain_column
    )

    value_sum = dot(mixed_low, first_low, NN)
    key_sum = dot((partial_z * cross_scale).astype(BF16), hat_rows, NN)
    inputgain_part = jnp.sum(partial_gain, axis=1)
    value_sum = jnp.where(row_index == channels, crossnorm_grad[None], value_sum)
    value_sum = jnp.where(row_index == channels + 1, selfnorm_grad[None], value_sum)
    value_sum = jnp.where(row_index == channels + 2, mlpnorm_grad[None], value_sum)
    wide_gain = jnp.pad(inputgain_part, (0, width - rows))
    key_sum = jnp.where(row_index == channels, wide_gain[None], key_sum)
    shared, partial_z, cross_pair = reduced_everywhere(
        jnp.concatenate([value_sum, key_sum], axis=0), partial_z, cross_pair
    )
    crossup_grad, crossdown_grad = scattered_pair(cross_pair)
    value_sum, key_sum = shared[:rows], shared[rows:]

    z_blocks = jnp.split(partial_z, group, axis=1)
    z_parts = exchanged([z_blocks[0]] + [part.astype(BF16) for part in z_blocks[1:]])
    z_own = (sum(part.astype(F32) for part in z_parts) * cross_scale).astype(BF16)
    latent_normed_grad = dot(z_own, key_map, TN)
    latent_input_grad, _ = norm_backward(latent_hat, latent_scale, latentgain, latent_normed_grad)
    latents_grad = first_grad + latent_input_grad

    inputgain_grad = key_sum[channels, :channels].astype(F32)
    crossnorm_grad = value_sum[channels].astype(F32)
    selfnorm_grad = value_sum[channels + 1].astype(F32)
    mlpnorm_grad = value_sum[channels + 2].astype(F32)
    value_sum, key_sum = value_sum[:channels], key_sum[:channels]
    latentgain_grad = jnp.sum(
        key_map[:channels].astype(F32) * key_sum.astype(F32), axis=0
    )
    key_scaled = (key_sum.astype(F32) * latentgain).astype(BF16)
    crossquery_grad = dot(key_scaled, crosskey, TN)
    crosskey_grad = dot(key_scaled, crossquery, NN)
    crossoutput_grad = dot(crossvalue, value_sum, TN)
    crossvalue_grad = dot(value_sum, crossoutput, NT)

    return (
        latents_out[None],
        latents_grad[None],
        jnp.transpose(inputs_grad, (1, 2, 0)),
        latentgain_grad,
        inputgain_grad,
        crossquery_grad,
        crosskey_grad,
        crossvalue_grad,
        crossoutput_grad,
        crossnorm_grad,
        crossup_grad,
        crossdown_grad,
        selfnorm_grad,
        query_grad,
        key_grad,
        value_grad,
        output_grad.T,
        mlpnorm_grad,
        selfup_grad,
        selfdown_grad,
    )


def solution(mesh):
    rows = P("dp", "mp", None)
    columns = P(None, "mp")
    outer = P("mp", None)
    whole = P()
    split = P("dp", "mp")
    turned = P("mp", "dp")
    return jax.shard_map(
        shards,
        mesh=mesh,
        in_specs=(
            rows,
            rows,
            P("dp"),
            whole,
            whole,
            whole,
            whole,
            whole,
            whole,
            whole,
            columns,
            outer,
            whole,
            columns,
            columns,
            columns,
            outer,
            whole,
            columns,
            outer,
            rows,
        ),
        out_specs=(
            rows,
            rows,
            rows,
            whole,
            whole,
            whole,
            whole,
            whole,
            whole,
            whole,
            split,
            turned,
            whole,
            split,
            split,
            split,
            turned,
            whole,
            split,
            turned,
        ),
        check_vma=False,
    )
```

```python
import functools

import jax
import jax.numpy as jnp
from jax import lax
from jax.experimental.layout import Layout, with_layout_constraint
from jax.experimental import pallas as pl
from jax.experimental.pallas import tpu as pltpu
from jax.sharding import PartitionSpec as P

HEADS = 8
EPSILON = 1e-05
MASKED = -1e30
FLOOR = -1e25
TILE = 1152
VMEM_LIMIT = 60 * 1024 * 1024
BF16 = jnp.bfloat16
F32 = jnp.float32
NN = (((1,), (0,)), ((), ()))
NT = (((1,), (1,)), ((), ()))
TN = (((0,), (0,)), ((), ()))


def dot(left, right, dims):
    return lax.dot_general(left, right, dims, preferred_element_type=F32)


def padded_rows(channels):
    return -(-(channels + 3) // 16) * 16


def normalized(raw_ref, channels, head_rows):
    top = raw_ref[:head_rows, :].astype(F32)
    rest = raw_ref[head_rows:, :].astype(F32)
    keep = lax.broadcasted_iota(jnp.int32, rest.shape, 0) < (channels - head_rows)
    rest = jnp.where(keep, rest, 0.0)
    mean = (jnp.sum(top, 0, keepdims=True) + jnp.sum(rest, 0, keepdims=True)) * (1.0 / channels)
    top = top - mean
    rest = jnp.where(keep, rest - mean, 0.0)
    square = jnp.sum(top * top, 0, keepdims=True) + jnp.sum(rest * rest, 0, keepdims=True)
    scale = lax.rsqrt(square * (1.0 / channels) + EPSILON)
    return top * scale, rest * scale, scale, keep


def prepare_kernel(limit_ref, raw_ref, gain_ref, out_ref, *, channels, head_rows):
    top, rest, _, keep = normalized(raw_ref, channels, head_rows)
    out_ref[:head_rows, :] = (top * gain_ref[:head_rows, :]).astype(BF16)
    lane = pl.program_id(0) * TILE + lax.broadcasted_iota(jnp.int32, rest.shape, 1)
    row = lax.broadcasted_iota(jnp.int32, rest.shape, 0) + head_rows
    invalid = jnp.where(lane < limit_ref[0], 0.0, 1.0)
    ones = (row == channels) | (row == channels + 2)
    extra = jnp.where(row == channels + 1, invalid, jnp.where(ones, 1.0, 0.0))
    out_ref[head_rows:, :] = jnp.where(keep, rest * gain_ref[head_rows:, :], extra).astype(BF16)


def prepare(limit, raw, gain_column):
    channels, count = raw.shape
    rows = padded_rows(channels)
    tiles = pl.cdiv(count, TILE)
    return pl.pallas_call(
        functools.partial(prepare_kernel, channels=channels, head_rows=rows - 16),
        grid_spec=pltpu.PrefetchScalarGridSpec(
            num_scalar_prefetch=1,
            grid=(tiles,),
            in_specs=[
                pl.BlockSpec((rows, TILE), lambda i, _: (0, i)),
                pl.BlockSpec((rows, 1), lambda i, _: (0, 0)),
            ],
            out_specs=pl.BlockSpec((rows, TILE), lambda i, _: (0, i)),
        ),
        out_shape=jax.ShapeDtypeStruct((rows, tiles * TILE), BF16),
        compiler_params=pltpu.CompilerParams(vmem_limit_bytes=VMEM_LIMIT),
        name="prepare",
    )(limit, raw, gain_column)


def forward_kernel(x_ref, a_ref, p_ref, y_ref, top_ref, running):
    @pl.when(pl.program_id(0) == 0)
    def _():
        running[...] = jnp.full_like(running, FLOOR)
        y_ref[...] = jnp.zeros_like(y_ref)

    x = x_ref[...]
    scores = dot(x, a_ref[...], TN)
    old = running[0:1, :]
    new = jnp.maximum(old, jnp.max(scores, 0, keepdims=True))
    probs = jnp.exp(scores - new).astype(BF16)
    p_ref[...] = probs
    y_ref[...] = y_ref[...] * jnp.exp(old - new) + dot(x, probs, NN)
    running[0:1, :] = new
    top_ref[0] = new


def cross_forward(x, a):
    rows, count = x.shape
    queries = a.shape[1]
    tiles = count // TILE
    return pl.pallas_call(
        forward_kernel,
        grid=(tiles,),
        in_specs=[
            pl.BlockSpec((rows, TILE), lambda i: (0, i)),
            pl.BlockSpec((rows, queries), lambda i: (0, 0)),
        ],
        out_specs=[
            pl.BlockSpec((TILE, queries), lambda i: (i, 0)),
            pl.BlockSpec((rows, queries), lambda i: (0, 0)),
            pl.BlockSpec((1, 1, queries), lambda i: (i, 0, 0)),
        ],
        out_shape=[
            jax.ShapeDtypeStruct((count, queries), BF16),
            jax.ShapeDtypeStruct((rows, queries), F32),
            jax.ShapeDtypeStruct((tiles, 1, queries), F32),
        ],
        scratch_shapes=[pltpu.VMEM((8, queries), F32)],
        compiler_params=pltpu.CompilerParams(vmem_limit_bytes=VMEM_LIMIT),
        name="cross_forward",
    )(x, a)


def lane_sums(values):
    total = values[:, :128]
    for k in range(1, values.shape[1] // 128):
        total = total + values[:, 128 * k : 128 * (k + 1)]
    return total


def backward_kernel(
    limit_ref,
    raw_ref,
    x_ref,
    p_ref,
    factor_ref,
    a_ref,
    b_ref,
    gain_ref,
    out_ref,
    z_ref,
    gain_grad_ref,
    *,
    channels,
    head_rows,
    guard,
):
    @pl.when(pl.program_id(0) == 0)
    def _():
        z_ref[...] = jnp.zeros_like(z_ref)
        gain_grad_ref[...] = jnp.zeros_like(gain_grad_ref)

    x = x_ref[...]
    slope = dot(x, b_ref[...], TN)
    probs = p_ref[...].astype(F32) * factor_ref[0]
    score_grad = (probs * slope).astype(BF16)
    probs = probs.astype(BF16)
    z_ref[...] += dot(x, score_grad, NN)
    grad = dot(a_ref[...], score_grad, NT) + dot(b_ref[...], probs, NT)
    top, rest, scale, keep = normalized(raw_ref, channels, head_rows)
    grad_top = grad[:head_rows]
    grad_rest = jnp.where(keep, grad[head_rows:], 0.0)
    if guard:
        lane = pl.program_id(0) * TILE + lax.broadcasted_iota(jnp.int32, (1, TILE), 1)
        inside = lane < limit_ref[0]
        grad_top = jnp.where(inside, grad_top, 0.0)
        grad_rest = jnp.where(inside, grad_rest, 0.0)
        top = jnp.where(inside, top, 0.0)
        rest = jnp.where(inside, rest, 0.0)
        scale = jnp.where(inside, scale, 0.0)
    gain_grad_ref[:head_rows, :] += lane_sums(grad_top * top)
    gain_grad_ref[head_rows:, :] += lane_sums(grad_rest * rest)
    grad_top = grad_top * gain_ref[:head_rows, :]
    grad_rest = grad_rest * gain_ref[head_rows:, :]
    mean = jnp.sum(grad_top, 0, keepdims=True) + jnp.sum(grad_rest, 0, keepdims=True)
    along = jnp.sum(grad_top * top, 0, keepdims=True) + jnp.sum(grad_rest * rest, 0, keepdims=True)
    mean = mean * (1.0 / channels)
    along = along * (1.0 / channels)
    out_ref[:head_rows, 0, :] = (grad_top - mean - top * along) * scale
    out_rest = (grad_rest - mean - rest * along) * scale
    out_ref[head_rows:, 0, :] = out_rest[: channels - head_rows]


def cross_backward(limit, raw, x, probs, factor, a, b, gain_column):
    channels, real = raw.shape
    rows, count = x.shape
    queries = a.shape[1]
    tiles = count // TILE
    return pl.pallas_call(
        functools.partial(
            backward_kernel, channels=channels, head_rows=rows - 16, guard=count != real
        ),
        grid_spec=pltpu.PrefetchScalarGridSpec(
            num_scalar_prefetch=1,
            grid=(tiles,),
            in_specs=[
                pl.BlockSpec((rows, TILE), lambda i, _: (0, i)),
                pl.BlockSpec((rows, TILE), lambda i, _: (0, i)),
                pl.BlockSpec((TILE, queries), lambda i, _: (i, 0)),
                pl.BlockSpec((1, 1, queries), lambda i, _: (i, 0, 0)),
                pl.BlockSpec((rows, queries), lambda i, _: (0, 0)),
                pl.BlockSpec((rows, queries), lambda i, _: (0, 0)),
                pl.BlockSpec((rows, 1), lambda i, _: (0, 0)),
            ],
            out_specs=[
                pl.BlockSpec((channels, 1, TILE), lambda i, _: (0, 0, i)),
                pl.BlockSpec((rows, queries), lambda i, _: (0, 0)),
                pl.BlockSpec((rows, 128), lambda i, _: (0, 0)),
            ],
        ),
        out_shape=[
            jax.ShapeDtypeStruct((channels, 1, real), F32),
            jax.ShapeDtypeStruct((rows, queries), F32),
            jax.ShapeDtypeStruct((rows, 128), F32),
        ],
        compiler_params=pltpu.CompilerParams(vmem_limit_bytes=VMEM_LIMIT),
        name="cross_backward",
    )(limit, raw, x, probs, factor, a, b, gain_column)


def shifted(block, distance):
    size = lax.axis_size("mp")
    return lax.ppermute(block, "mp", [(i, (i + distance) % size) for i in range(size)])


def gathered(block):
    size = lax.axis_size("mp")
    return [block] + [shifted(block, d) for d in range(1, size)]


def exchanged(blocks):
    return [blocks[0]] + [shifted(blocks[d], -d) for d in range(1, len(blocks))]


def summed_rows(partial):
    size = lax.axis_size("mp")
    blocks = jnp.split(partial, size, axis=0)
    sent = [blocks[0]] + [block.astype(BF16) for block in blocks[1:]]
    total = sent[0]
    for block in exchanged(sent)[1:]:
        total = total + block.astype(F32)
    return total


def reduced_everywhere(values, held, later):
    data, size = lax.axis_size("dp"), lax.axis_size("mp")
    index = lax.axis_index("dp")
    bits = [1 << k for k in range(data.bit_length() - 1)]
    for bit in bits:
        low, high = jnp.split(values, 2, axis=1)
        upper = (index & bit) != 0
        mine = jnp.where(upper, high, low)
        other = jnp.where(upper, low, high).astype(BF16)
        swap = [(i, i ^ bit) for i in range(data)]
        values = mine + lax.ppermute(other, "dp", swap).astype(F32)
        if bit == bits[0]:
            values, held = lax.optimization_barrier((values, held))
    rows, columns = values.shape
    chunks = values.reshape(size, rows // size, columns)
    place = lax.axis_index("mp")

    def chunk(k):
        return lax.dynamic_index_in_dim(chunks, (place + k) % size, 0, keepdims=False)

    total = chunk(0)
    for d in range(1, size):
        total = total + shifted(chunk(d).astype(BF16), d).astype(F32)
    own = total.astype(BF16)
    full = jnp.zeros((size,) + own.shape, BF16)
    for d, block in enumerate(gathered(own)):
        full = lax.dynamic_update_index_in_dim(full, block, (place - d) % size, 0)
    full = full.reshape(rows, columns)
    full, later = lax.optimization_barrier((full, later))
    for bit in reversed(bits):
        swap = [(i, i ^ bit) for i in range(data)]
        other = lax.ppermute(full, "dp", swap)
        upper = (index & bit) != 0
        full = jnp.where(
            upper, jnp.concatenate([other, full], 1), jnp.concatenate([full, other], 1)
        )
    return full, held, later


def standardized(values):
    centred = values - jnp.mean(values, axis=-1, keepdims=True)
    spread = jnp.mean(centred * centred, axis=-1, keepdims=True)
    scale = lax.rsqrt(spread + EPSILON)
    return centred * scale, scale


def norm_backward(hat, scale, gain, upstream):
    weighted = upstream * gain
    mean = jnp.mean(weighted, axis=-1, keepdims=True)
    along = jnp.mean(weighted * hat, axis=-1, keepdims=True)
    return (weighted - mean - hat * along) * scale, jnp.sum(upstream * hat, axis=0)


def gelu_tanh(values):
    return jax.nn.gelu(values, approximate=True)


def gelu_backward(values, upstream):
    return jax.vjp(gelu_tanh, values)[1](upstream)[0]


def whole_weights(up, down):
    data = lax.axis_size("dp")
    index = lax.axis_index("dp")
    pair = jnp.stack([up.T, down])
    part = pair.shape[1] // data
    piece = lax.dynamic_slice_in_dim(pair, index * part, part, 1)
    full = lax.all_gather(piece, ("mp", "dp"), axis=1, tiled=True)
    return full[0], full[1]


def mlp_forward(residual, gain, up, down):
    hat, scale = standardized(residual)
    normed = (hat * gain).astype(BF16)
    hidden = dot(normed, up, NT)
    active = gelu_tanh(hidden).astype(BF16)
    return residual + dot(active, down, NN), (hat, scale, normed, hidden, active)


def mlp_backward(upstream, gain, up, down, stored):
    hat, scale, normed, hidden, active = stored
    low = upstream.astype(BF16)
    active_grad = dot(low, down, NT)
    hidden_grad = gelu_backward(hidden, active_grad).astype(BF16)
    normed_grad = dot(hidden_grad, up, NN)
    input_grad, gain_grad = norm_backward(hat, scale, gain, normed_grad)
    return upstream + input_grad, gain_grad, (normed, hidden_grad, low, active)


def pair_gradients(operands):
    normed, hidden_grad, low, active = operands
    size = lax.axis_size("mp")
    grads = (dot(hidden_grad, normed, TN).T, dot(active, low, TN).T)
    pieces = [jnp.split(grad.astype(BF16), size, axis=1) for grad in grads]
    return row_major(jnp.concatenate([piece[k] for k in range(size) for piece in pieces], axis=1))


def row_major(values):
    return with_layout_constraint(values, Layout((0, 1)))


def summed_over_images(stacked):
    return lax.psum_scatter(stacked, "dp", scatter_dimension=0, tiled=True)


def scattered_pair(mine):
    size = lax.axis_size("mp")
    part = mine.shape[1] // size
    place = lax.axis_index("mp")

    def chunk(k):
        return lax.dynamic_slice_in_dim(mine, (place + k) % size * part, part, 1)

    total = chunk(0).astype(F32)
    for d in range(1, size):
        total = total + shifted(chunk(d), d).astype(F32)
    first, second = jnp.split(total, 2, axis=1)
    return first, second.T


def shards(
    latents,
    inputs,
    image_sizes,
    latentgain,
    inputgain,
    crossquery,
    crosskey,
    crossvalue,
    crossoutput,
    crossnorm,
    crossup,
    crossdown,
    selfnorm,
    selfquery,
    selfkey,
    selfvalue,
    selfoutput,
    mlpnorm,
    selfup,
    selfdown,
    cotangent,
):
    width = latents.shape[-1]
    channels = inputs.shape[-1]
    count = inputs.shape[1]
    head_size = width // HEADS
    rows = padded_rows(channels)
    group = lax.axis_size("mp")
    cross_scale = width**-0.5
    self_scale = head_size**-0.5

    cross_up, cross_down = whole_weights(crossup, crossdown)
    self_up, self_down = whole_weights(selfup, selfdown)

    latent_float = latents[0].astype(F32)
    padding = ((0, rows - channels), (0, 0))
    key_weight = jnp.pad(crosskey, padding)
    value_weight = jnp.pad(crossvalue, padding)
    key_map = dot(key_weight, crossquery, NT).astype(BF16)
    value_map = dot(value_weight, crossoutput, NN).astype(BF16)

    latent_hat, latent_scale = standardized(latent_float)
    normed_latent = (latent_hat * latentgain).astype(BF16)
    row_index = lax.broadcasted_iota(jnp.int32, (rows, 1), 0)
    score_map = dot(key_map, normed_latent, NT) * cross_scale
    score_map = jnp.where(row_index == channels + 1, MASKED, score_map).astype(BF16)
    score_maps = jnp.concatenate(gathered(score_map), axis=1)
    hat_rows = jnp.concatenate(gathered(latent_hat.astype(BF16)), axis=0)

    limit = jnp.clip(image_sizes - lax.axis_index("mp") * count, 0, count)
    extent = jnp.full((1,), count, jnp.int32)
    raw = inputs[0].T
    gain_column = jnp.pad(inputgain[:, None], padding)
    x = prepare(limit, raw, gain_column)
    probs, partial, tops = cross_forward(x, score_maps)

    partial = jnp.where(row_index == channels + 1, tops[-1], partial)
    parts = exchanged(jnp.split(partial, group, axis=1))
    part_tops = [part[channels + 1 : channels + 2] for part in parts]
    top = functools.reduce(jnp.maximum, part_tops)
    mixed = sum(part * jnp.exp(part_top - top) for part, part_top in zip(parts, part_tops))
    total = mixed[channels : channels + 1]
    log_total = top + jnp.log(total)
    mixed = jnp.where(row_index < channels, mixed / total, 0.0)
    log_all = jnp.concatenate(gathered(log_total), axis=1)
    mixed_low = mixed.astype(BF16)

    first_resid = latent_float + dot(mixed_low, value_map, TN)
    second_resid, cross_stored = mlp_forward(first_resid, crossnorm, cross_up, cross_down)

    self_hat, self_norm_scale = standardized(second_resid)
    normed_self = (self_hat * selfnorm).astype(BF16)
    normed_self, log_all = lax.optimization_barrier((normed_self, log_all))
    factor = jnp.exp(tops - log_all[None])
    self_rows = jnp.concatenate(gathered(normed_self), axis=0)
    tokens = self_rows.shape[0]
    projections = jnp.concatenate([selfquery, selfkey, selfvalue], axis=1)
    block = selfquery.shape[1]
    projected = dot(self_rows, projections, NN).astype(BF16)

    def heads_of(flat):
        return flat.reshape(tokens, -1, head_size)

    queries, keys, values = (
        heads_of(projected[:, k * block : (k + 1) * block]) for k in range(3)
    )

    def product(pattern, left, right):
        return jnp.einsum(pattern, left, right, preferred_element_type=F32)

    scores = product("qhe,khe->hqk", queries, keys) * self_scale
    self_top = jnp.max(scores, axis=-1, keepdims=True)
    powers = jnp.exp(scores - self_top)
    self_probs = powers / jnp.sum(powers, axis=-1, keepdims=True)
    self_low = self_probs.astype(BF16)
    attended = product("hqk,khe->qhe", self_low, values).reshape(tokens, -1).astype(BF16)
    third_resid = second_resid + summed_rows(dot(attended, selfoutput, NN))
    final_resid, self_stored = mlp_forward(third_resid, mlpnorm, self_up, self_down)
    latents_out = final_resid.astype(BF16)

    upstream = cotangent[0].astype(F32)
    third_grad, mlpnorm_grad, self_pair = mlp_backward(
        upstream, mlpnorm, self_up, self_down, self_stored
    )
    third_low, self_pair = lax.optimization_barrier((third_grad.astype(BF16), self_pair))
    third_rows = jnp.concatenate(gathered(third_low), axis=0)
    third_rows, self_pair = lax.optimization_barrier((third_rows, pair_gradients(self_pair)))
    self_pair = summed_over_images(self_pair)
    attended_grad = heads_of(dot(third_rows, selfoutput, NT).astype(BF16))
    self_probs_grad = product("qhe,khe->hqk", attended_grad, values)
    self_row = jnp.sum(self_probs * self_probs_grad, axis=-1, keepdims=True)
    scores_grad = (self_probs * (self_probs_grad - self_row) * self_scale).astype(BF16)
    values_grad = product("hqk,qhe->khe", self_low, attended_grad)
    queries_grad = product("hqk,khe->qhe", scores_grad, keys)
    keys_grad = product("hqk,qhe->khe", scores_grad, queries)
    projected_grad = jnp.concatenate(
        [grad.reshape(tokens, -1).astype(BF16) for grad in (queries_grad, keys_grad, values_grad)],
        axis=1,
    )
    normed_part = dot(projected_grad, projections, NT)
    normed_part, sources = lax.optimization_barrier(
        (normed_part, (self_rows, projected_grad, third_rows, attended))
    )
    normed_self_grad = summed_rows(normed_part)
    attention_grads = jnp.concatenate(
        [dot(sources[1], sources[0], TN).T, dot(sources[3], sources[2], TN).T], axis=1
    )
    attention_grads = row_major(attention_grads.astype(BF16))
    normed_self_grad, attention_grads = lax.optimization_barrier(
        (normed_self_grad, attention_grads)
    )
    attention_grads = summed_over_images(attention_grads).astype(F32)
    query_grad, key_grad, value_grad, output_grad = jnp.split(attention_grads, 4, axis=1)

    second_input_grad, selfnorm_grad = norm_backward(
        self_hat, self_norm_scale, selfnorm, normed_self_grad
    )
    second_grad = third_grad + second_input_grad
    first_grad, crossnorm_grad, cross_pair = mlp_backward(
        second_grad, crossnorm, cross_up, cross_down, cross_stored
    )
    first_low = first_grad.astype(BF16)
    slope_map = dot(value_map, first_low, NT).astype(BF16)
    offset = -jnp.sum(slope_map.astype(F32) * mixed, axis=0, keepdims=True)
    offset_high = offset.astype(BF16)
    offset_low = (offset - offset_high.astype(F32)).astype(BF16)
    slope_map = jnp.where(row_index == channels, offset_high, slope_map)
    slope_map = jnp.where(row_index == channels + 2, offset_low, slope_map)
    slope_map, cross_pair = lax.optimization_barrier((slope_map, cross_pair))
    slope_maps = jnp.concatenate(gathered(slope_map), axis=1)
    slope_maps, cross_pair, self_pair = lax.optimization_barrier(
        (slope_maps, pair_gradients(cross_pair), self_pair)
    )
    cross_pair = summed_over_images(cross_pair)
    selfup_grad, selfdown_grad = scattered_pair(self_pair)
    inputs_grad, partial_z, partial_gain = cross_backward(
        extent, raw, x, probs, factor, score_maps, slope_maps, gain_column
    )

    value_sum = dot(mixed_low, first_low, NN)
    key_sum = dot((partial_z * cross_scale).astype(BF16), hat_rows, NN)
    inputgain_part = jnp.sum(partial_gain, axis=1)
    value_sum = jnp.where(row_index == channels, crossnorm_grad[None], value_sum)
    value_sum = jnp.where(row_index == channels + 1, selfnorm_grad[None], value_sum)
    value_sum = jnp.where(row_index == channels + 2, mlpnorm_grad[None], value_sum)
    wide_gain = jnp.pad(inputgain_part, (0, width - rows))
    key_sum = jnp.where(row_index == channels, wide_gain[None], key_sum)
    shared, partial_z, cross_pair = reduced_everywhere(
        jnp.concatenate([value_sum, key_sum], axis=0), partial_z, cross_pair
    )
    crossup_grad, crossdown_grad = scattered_pair(cross_pair)
    value_sum, key_sum = shared[:rows], shared[rows:]

    z_blocks = jnp.split(partial_z, group, axis=1)
    z_parts = exchanged([z_blocks[0]] + [part.astype(BF16) for part in z_blocks[1:]])
    z_own = (sum(part.astype(F32) for part in z_parts) * cross_scale).astype(BF16)
    latent_normed_grad = dot(z_own, key_map, TN)
    latent_input_grad, _ = norm_backward(latent_hat, latent_scale, latentgain, latent_normed_grad)
    latents_grad = first_grad + latent_input_grad

    inputgain_grad = key_sum[channels, :channels].astype(F32)
    crossnorm_grad = value_sum[channels].astype(F32)
    selfnorm_grad = value_sum[channels + 1].astype(F32)
    mlpnorm_grad = value_sum[channels + 2].astype(F32)
    value_sum, key_sum = value_sum[:channels], key_sum[:channels]
    latentgain_grad = jnp.sum(
        key_map[:channels].astype(F32) * key_sum.astype(F32), axis=0
    )
    key_scaled = (key_sum.astype(F32) * latentgain).astype(BF16)
    crossquery_grad = row_major(dot(key_scaled, crosskey, TN))
    crosskey_grad = dot(key_scaled, crossquery, NN)
    crossoutput_grad = dot(crossvalue, value_sum, TN)
    crossvalue_grad = dot(value_sum, crossoutput, NT)

    return (
        latents_out[None],
        latents_grad[None],
        jnp.transpose(inputs_grad, (1, 2, 0)),
        latentgain_grad,
        inputgain_grad,
        crossquery_grad,
        crosskey_grad,
        crossvalue_grad,
        crossoutput_grad,
        crossnorm_grad,
        crossup_grad,
        crossdown_grad,
        selfnorm_grad,
        query_grad,
        key_grad,
        value_grad,
        output_grad.T,
        mlpnorm_grad,
        selfup_grad,
        selfdown_grad,
    )


def solution(mesh):
    rows = P("dp", "mp", None)
    columns = P(None, "mp")
    outer = P("mp", None)
    whole = P()
    split = P("dp", "mp")
    turned = P("mp", "dp")
    return jax.shard_map(
        shards,
        mesh=mesh,
        in_specs=(
            rows,
            rows,
            P("dp"),
            whole,
            whole,
            whole,
            whole,
            whole,
            whole,
            whole,
            columns,
            outer,
            whole,
            columns,
            columns,
            columns,
            outer,
            whole,
            columns,
            outer,
            rows,
        ),
        out_specs=(
            rows,
            rows,
            rows,
            whole,
            whole,
            whole,
            whole,
            whole,
            whole,
            whole,
            split,
            turned,
            whole,
            split,
            split,
            split,
            turned,
            whole,
            split,
            turned,
        ),
        check_vma=False,
    )
```

```python
import functools

import jax
import jax.numpy as jnp
from jax import lax
from jax.experimental.layout import Layout, with_layout_constraint
from jax.experimental import pallas as pl
from jax.experimental.pallas import tpu as pltpu
from jax.sharding import PartitionSpec as P

HEADS = 8
EPSILON = 1e-05
MASKED = -1e30
FLOOR = -1e25
TILE = 1152
VMEM_LIMIT = 60 * 1024 * 1024
BF16 = jnp.bfloat16
F32 = jnp.float32
NN = (((1,), (0,)), ((), ()))
NT = (((1,), (1,)), ((), ()))
TN = (((0,), (0,)), ((), ()))


def dot(left, right, dims):
    return lax.dot_general(left, right, dims, preferred_element_type=F32)


def padded_rows(channels):
    return -(-(channels + 3) // 16) * 16


def normalized(raw_ref, channels, head_rows):
    top = raw_ref[:head_rows, :].astype(F32)
    rest = raw_ref[head_rows:, :].astype(F32)
    keep = lax.broadcasted_iota(jnp.int32, rest.shape, 0) < (channels - head_rows)
    rest = jnp.where(keep, rest, 0.0)
    mean = (jnp.sum(top, 0, keepdims=True) + jnp.sum(rest, 0, keepdims=True)) * (1.0 / channels)
    top = top - mean
    rest = jnp.where(keep, rest - mean, 0.0)
    square = jnp.sum(top * top, 0, keepdims=True) + jnp.sum(rest * rest, 0, keepdims=True)
    scale = lax.rsqrt(square * (1.0 / channels) + EPSILON)
    return top * scale, rest * scale, scale, keep


def prepare_kernel(limit_ref, raw_ref, gain_ref, out_ref, *, channels, head_rows):
    top, rest, _, keep = normalized(raw_ref, channels, head_rows)
    out_ref[:head_rows, :] = (top * gain_ref[:head_rows, :]).astype(BF16)
    lane = pl.program_id(0) * TILE + lax.broadcasted_iota(jnp.int32, rest.shape, 1)
    row = lax.broadcasted_iota(jnp.int32, rest.shape, 0) + head_rows
    invalid = jnp.where(lane < limit_ref[0], 0.0, 1.0)
    ones = (row == channels) | (row == channels + 2)
    extra = jnp.where(row == channels + 1, invalid, jnp.where(ones, 1.0, 0.0))
    out_ref[head_rows:, :] = jnp.where(keep, rest * gain_ref[head_rows:, :], extra).astype(BF16)


def prepare(limit, raw, gain_column):
    channels, count = raw.shape
    rows = padded_rows(channels)
    tiles = pl.cdiv(count, TILE)
    return pl.pallas_call(
        functools.partial(prepare_kernel, channels=channels, head_rows=rows - 16),
        grid_spec=pltpu.PrefetchScalarGridSpec(
            num_scalar_prefetch=1,
            grid=(tiles,),
            in_specs=[
                pl.BlockSpec((rows, TILE), lambda i, _: (0, i)),
                pl.BlockSpec((rows, 1), lambda i, _: (0, 0)),
            ],
            out_specs=pl.BlockSpec((rows, TILE), lambda i, _: (0, i)),
        ),
        out_shape=jax.ShapeDtypeStruct((rows, tiles * TILE), BF16),
        compiler_params=pltpu.CompilerParams(vmem_limit_bytes=VMEM_LIMIT),
        name="prepare",
    )(limit, raw, gain_column)


def forward_kernel(x_ref, a_ref, p_ref, y_ref, top_ref, running):
    @pl.when(pl.program_id(0) == 0)
    def _():
        running[...] = jnp.full_like(running, FLOOR)
        y_ref[...] = jnp.zeros_like(y_ref)

    x = x_ref[...]
    scores = dot(x, a_ref[...], TN)
    old = running[0:1, :]
    new = jnp.maximum(old, jnp.max(scores, 0, keepdims=True))
    probs = jnp.exp(scores - new).astype(BF16)
    p_ref[...] = probs
    y_ref[...] = y_ref[...] * jnp.exp(old - new) + dot(x, probs, NN)
    running[0:1, :] = new
    top_ref[0] = new


def cross_forward(x, a):
    rows, count = x.shape
    queries = a.shape[1]
    tiles = count // TILE
    return pl.pallas_call(
        forward_kernel,
        grid=(tiles,),
        in_specs=[
            pl.BlockSpec((rows, TILE), lambda i: (0, i)),
            pl.BlockSpec((rows, queries), lambda i: (0, 0)),
        ],
        out_specs=[
            pl.BlockSpec((TILE, queries), lambda i: (i, 0)),
            pl.BlockSpec((rows, queries), lambda i: (0, 0)),
            pl.BlockSpec((1, 1, queries), lambda i: (i, 0, 0)),
        ],
        out_shape=[
            jax.ShapeDtypeStruct((count, queries), BF16),
            jax.ShapeDtypeStruct((rows, queries), F32),
            jax.ShapeDtypeStruct((tiles, 1, queries), F32),
        ],
        scratch_shapes=[pltpu.VMEM((8, queries), F32)],
        compiler_params=pltpu.CompilerParams(vmem_limit_bytes=VMEM_LIMIT),
        name="cross_forward",
    )(x, a)


def lane_sums(values):
    total = values[:, :128]
    for k in range(1, values.shape[1] // 128):
        total = total + values[:, 128 * k : 128 * (k + 1)]
    return total


def backward_kernel(
    limit_ref,
    raw_ref,
    x_ref,
    p_ref,
    factor_ref,
    a_ref,
    b_ref,
    gain_ref,
    out_ref,
    z_ref,
    gain_grad_ref,
    *,
    channels,
    head_rows,
    guard,
):
    @pl.when(pl.program_id(0) == 0)
    def _():
        z_ref[...] = jnp.zeros_like(z_ref)
        gain_grad_ref[...] = jnp.zeros_like(gain_grad_ref)

    x = x_ref[...]
    slope = dot(x, b_ref[...], TN)
    probs = p_ref[...].astype(F32) * factor_ref[0]
    score_grad = (probs * slope).astype(BF16)
    probs = probs.astype(BF16)
    z_ref[...] += dot(x, score_grad, NN)
    grad = dot(a_ref[...], score_grad, NT) + dot(b_ref[...], probs, NT)
    top, rest, scale, keep = normalized(raw_ref, channels, head_rows)
    grad_top = grad[:head_rows]
    grad_rest = jnp.where(keep, grad[head_rows:], 0.0)
    if guard:
        lane = pl.program_id(0) * TILE + lax.broadcasted_iota(jnp.int32, (1, TILE), 1)
        inside = lane < limit_ref[0]
        grad_top = jnp.where(inside, grad_top, 0.0)
        grad_rest = jnp.where(inside, grad_rest, 0.0)
        top = jnp.where(inside, top, 0.0)
        rest = jnp.where(inside, rest, 0.0)
        scale = jnp.where(inside, scale, 0.0)
    gain_grad_ref[:head_rows, :] += lane_sums(grad_top * top)
    gain_grad_ref[head_rows:, :] += lane_sums(grad_rest * rest)
    grad_top = grad_top * gain_ref[:head_rows, :]
    grad_rest = grad_rest * gain_ref[head_rows:, :]
    mean = jnp.sum(grad_top, 0, keepdims=True) + jnp.sum(grad_rest, 0, keepdims=True)
    along = jnp.sum(grad_top * top, 0, keepdims=True) + jnp.sum(grad_rest * rest, 0, keepdims=True)
    mean = mean * (1.0 / channels)
    along = along * (1.0 / channels)
    out_ref[:head_rows, 0, :] = (grad_top - mean - top * along) * scale
    out_rest = (grad_rest - mean - rest * along) * scale
    out_ref[head_rows:, 0, :] = out_rest[: channels - head_rows]


def cross_backward(limit, raw, x, probs, factor, a, b, gain_column):
    channels, real = raw.shape
    rows, count = x.shape
    queries = a.shape[1]
    tiles = count // TILE
    return pl.pallas_call(
        functools.partial(
            backward_kernel, channels=channels, head_rows=rows - 16, guard=count != real
        ),
        grid_spec=pltpu.PrefetchScalarGridSpec(
            num_scalar_prefetch=1,
            grid=(tiles,),
            in_specs=[
                pl.BlockSpec((rows, TILE), lambda i, _: (0, i)),
                pl.BlockSpec((rows, TILE), lambda i, _: (0, i)),
                pl.BlockSpec((TILE, queries), lambda i, _: (i, 0)),
                pl.BlockSpec((1, 1, queries), lambda i, _: (i, 0, 0)),
                pl.BlockSpec((rows, queries), lambda i, _: (0, 0)),
                pl.BlockSpec((rows, queries), lambda i, _: (0, 0)),
                pl.BlockSpec((rows, 1), lambda i, _: (0, 0)),
            ],
            out_specs=[
                pl.BlockSpec((channels, 1, TILE), lambda i, _: (0, 0, i)),
                pl.BlockSpec((rows, queries), lambda i, _: (0, 0)),
                pl.BlockSpec((rows, 128), lambda i, _: (0, 0)),
            ],
        ),
        out_shape=[
            jax.ShapeDtypeStruct((channels, 1, real), F32),
            jax.ShapeDtypeStruct((rows, queries), F32),
            jax.ShapeDtypeStruct((rows, 128), F32),
        ],
        compiler_params=pltpu.CompilerParams(vmem_limit_bytes=VMEM_LIMIT),
        name="cross_backward",
    )(limit, raw, x, probs, factor, a, b, gain_column)


def shifted(block, distance):
    size = lax.axis_size("mp")
    return lax.ppermute(block, "mp", [(i, (i + distance) % size) for i in range(size)])


def gathered(block):
    size = lax.axis_size("mp")
    return [block] + [shifted(block, d) for d in range(1, size)]


def exchanged(blocks):
    return [blocks[0]] + [shifted(blocks[d], -d) for d in range(1, len(blocks))]


def summed_rows(partial):
    size = lax.axis_size("mp")
    blocks = jnp.split(partial, size, axis=0)
    sent = [blocks[0]] + [block.astype(BF16) for block in blocks[1:]]
    total = sent[0]
    for block in exchanged(sent)[1:]:
        total = total + block.astype(F32)
    return total


def reduced_everywhere(values, held, later):
    data, size = lax.axis_size("dp"), lax.axis_size("mp")
    index = lax.axis_index("dp")
    bits = [1 << k for k in range(data.bit_length() - 1)]
    for bit in bits:
        low, high = jnp.split(values, 2, axis=1)
        upper = (index & bit) != 0
        mine = jnp.where(upper, high, low)
        other = jnp.where(upper, low, high).astype(BF16)
        swap = [(i, i ^ bit) for i in range(data)]
        values = mine + lax.ppermute(other, "dp", swap).astype(F32)
        if bit == bits[0]:
            values, held = lax.optimization_barrier((values, held))
    rows, columns = values.shape
    chunks = values.reshape(size, rows // size, columns)
    place = lax.axis_index("mp")

    def chunk(k):
        return lax.dynamic_index_in_dim(chunks, (place + k) % size, 0, keepdims=False)

    total = chunk(0)
    for d in range(1, size):
        total = total + shifted(chunk(d).astype(BF16), d).astype(F32)
    own = total.astype(BF16)
    full = jnp.zeros((size,) + own.shape, BF16)
    for d, block in enumerate(gathered(own)):
        full = lax.dynamic_update_index_in_dim(full, block, (place - d) % size, 0)
    full = full.reshape(rows, columns)
    full, later = lax.optimization_barrier((full, later))
    for bit in reversed(bits):
        swap = [(i, i ^ bit) for i in range(data)]
        other = lax.ppermute(full, "dp", swap)
        upper = (index & bit) != 0
        full = jnp.where(
            upper, jnp.concatenate([other, full], 1), jnp.concatenate([full, other], 1)
        )
    return full, held, later


def standardized(values):
    centred = values - jnp.mean(values, axis=-1, keepdims=True)
    spread = jnp.mean(centred * centred, axis=-1, keepdims=True)
    scale = lax.rsqrt(spread + EPSILON)
    return centred * scale, scale


def norm_backward(hat, scale, gain, upstream):
    weighted = upstream * gain
    mean = jnp.mean(weighted, axis=-1, keepdims=True)
    along = jnp.mean(weighted * hat, axis=-1, keepdims=True)
    return (weighted - mean - hat * along) * scale, jnp.sum(upstream * hat, axis=0)


def gelu_tanh(values):
    return jax.nn.gelu(values, approximate=True)


def gelu_backward(values, upstream):
    return jax.vjp(gelu_tanh, values)[1](upstream)[0]


def whole_weights(up, down):
    data = lax.axis_size("dp")
    index = lax.axis_index("dp")
    pair = jnp.stack([up.T, down])
    part = pair.shape[1] // data
    piece = lax.dynamic_slice_in_dim(pair, index * part, part, 1)
    full = lax.all_gather(piece, ("mp", "dp"), axis=1, tiled=True)
    return full[0], full[1]


def mlp_forward(residual, gain, up, down):
    hat, scale = standardized(residual)
    normed = (hat * gain).astype(BF16)
    hidden = dot(normed, up, NT)
    active = gelu_tanh(hidden).astype(BF16)
    return residual + dot(active, down, NN), (hat, scale, normed, hidden, active)


def mlp_backward(upstream, gain, up, down, stored):
    hat, scale, normed, hidden, active = stored
    low = upstream.astype(BF16)
    active_grad = dot(low, down, NT)
    hidden_grad = gelu_backward(hidden, active_grad).astype(BF16)
    normed_grad = dot(hidden_grad, up, NN)
    input_grad, gain_grad = norm_backward(hat, scale, gain, normed_grad)
    return upstream + input_grad, gain_grad, (normed, hidden_grad, low, active)


def pair_gradients(operands):
    normed, hidden_grad, low, active = operands
    size = lax.axis_size("mp")
    grads = (dot(hidden_grad, normed, TN).T, dot(active, low, TN).T)
    pieces = [jnp.split(grad.astype(BF16), size, axis=1) for grad in grads]
    return row_major(jnp.concatenate([piece[k] for k in range(size) for piece in pieces], axis=1))


def row_major(values):
    return with_layout_constraint(values, Layout((0, 1)))


def summed_over_images(stacked):
    return lax.psum_scatter(stacked, "dp", scatter_dimension=0, tiled=True)


def scattered_pair(mine):
    size = lax.axis_size("mp")
    part = mine.shape[1] // size
    place = lax.axis_index("mp")

    def chunk(k):
        return lax.dynamic_slice_in_dim(mine, (place + k) % size * part, part, 1)

    total = chunk(0).astype(F32)
    for d in range(1, size):
        total = total + shifted(chunk(d), d).astype(F32)
    first, second = jnp.split(total, 2, axis=1)
    return first, second.T


def shards(
    latents,
    inputs,
    image_sizes,
    latentgain,
    inputgain,
    crossquery,
    crosskey,
    crossvalue,
    crossoutput,
    crossnorm,
    crossup,
    crossdown,
    selfnorm,
    selfquery,
    selfkey,
    selfvalue,
    selfoutput,
    mlpnorm,
    selfup,
    selfdown,
    cotangent,
):
    width = latents.shape[-1]
    channels = inputs.shape[-1]
    count = inputs.shape[1]
    head_size = width // HEADS
    rows = padded_rows(channels)
    group = lax.axis_size("mp")
    cross_scale = width**-0.5
    self_scale = head_size**-0.5

    cross_up, cross_down = whole_weights(crossup, crossdown)
    self_up, self_down = whole_weights(selfup, selfdown)

    latent_float = latents[0].astype(F32)
    padding = ((0, rows - channels), (0, 0))
    key_weight = jnp.pad(crosskey, padding)
    value_weight = jnp.pad(crossvalue, padding)
    key_map = dot(key_weight, crossquery, NT).astype(BF16)

    latent_hat, latent_scale = standardized(latent_float)
    normed_latent = (latent_hat * latentgain).astype(BF16)
    row_index = lax.broadcasted_iota(jnp.int32, (rows, 1), 0)
    score_map = dot(key_map, normed_latent, NT) * cross_scale
    score_map = jnp.where(row_index == channels + 1, MASKED, score_map).astype(BF16)
    score_maps = jnp.concatenate(gathered(score_map), axis=1)
    hat_rows = jnp.concatenate(gathered(latent_hat.astype(BF16)), axis=0)

    limit = jnp.clip(image_sizes - lax.axis_index("mp") * count, 0, count)
    extent = jnp.full((1,), count, jnp.int32)
    raw = inputs[0].T
    gain_column = jnp.pad(inputgain[:, None], padding)
    x = prepare(limit, raw, gain_column)
    probs, partial, tops = cross_forward(x, score_maps)

    partial = jnp.where(row_index == channels + 1, tops[-1], partial)
    partial, value_weight = lax.optimization_barrier((partial, value_weight))
    value_map = dot(value_weight, crossoutput, NN).astype(BF16)
    parts = exchanged(jnp.split(partial, group, axis=1))
    part_tops = [part[channels + 1 : channels + 2] for part in parts]
    top = functools.reduce(jnp.maximum, part_tops)
    mixed = sum(part * jnp.exp(part_top - top) for part, part_top in zip(parts, part_tops))
    total = mixed[channels : channels + 1]
    log_total = top + jnp.log(total)
    mixed = jnp.where(row_index < channels, mixed / total, 0.0)
    log_all = jnp.concatenate(gathered(log_total), axis=1)
    mixed_low = mixed.astype(BF16)

    first_resid = latent_float + dot(mixed_low, value_map, TN)
    second_resid, cross_stored = mlp_forward(first_resid, crossnorm, cross_up, cross_down)

    self_hat, self_norm_scale = standardized(second_resid)
    normed_self = (self_hat * selfnorm).astype(BF16)
    normed_self, log_all = lax.optimization_barrier((normed_self, log_all))
    factor = jnp.exp(tops - log_all[None])
    self_rows = jnp.concatenate(gathered(normed_self), axis=0)
    tokens = self_rows.shape[0]
    projections = jnp.concatenate([selfquery, selfkey, selfvalue], axis=1)
    block = selfquery.shape[1]
    projected = dot(self_rows, projections, NN).astype(BF16)

    def heads_of(flat):
        return flat.reshape(tokens, -1, head_size)

    queries, keys, values = (
        heads_of(projected[:, k * block : (k + 1) * block]) for k in range(3)
    )

    def product(pattern, left, right):
        return jnp.einsum(pattern, left, right, preferred_element_type=F32)

    scores = product("qhe,khe->hqk", queries, keys) * self_scale
    self_top = jnp.max(scores, axis=-1, keepdims=True)
    powers = jnp.exp(scores - self_top)
    self_probs = powers / jnp.sum(powers, axis=-1, keepdims=True)
    self_low = self_probs.astype(BF16)
    attended = product("hqk,khe->qhe", self_low, values).reshape(tokens, -1).astype(BF16)
    third_resid = second_resid + summed_rows(dot(attended, selfoutput, NN))
    final_resid, self_stored = mlp_forward(third_resid, mlpnorm, self_up, self_down)
    latents_out = final_resid.astype(BF16)

    upstream = cotangent[0].astype(F32)
    third_grad, mlpnorm_grad, self_pair = mlp_backward(
        upstream, mlpnorm, self_up, self_down, self_stored
    )
    third_low, self_pair = lax.optimization_barrier((third_grad.astype(BF16), self_pair))
    third_rows = jnp.concatenate(gathered(third_low), axis=0)
    third_rows, self_pair = lax.optimization_barrier((third_rows, pair_gradients(self_pair)))
    self_pair = summed_over_images(self_pair)
    attended_grad = heads_of(dot(third_rows, selfoutput, NT).astype(BF16))
    self_probs_grad = product("qhe,khe->hqk", attended_grad, values)
    self_row = jnp.sum(self_probs * self_probs_grad, axis=-1, keepdims=True)
    scores_grad = (self_probs * (self_probs_grad - self_row) * self_scale).astype(BF16)
    scores_grad = lax.optimization_barrier(scores_grad)
    values_grad = product("hqk,qhe->khe", self_low, attended_grad)
    queries_grad = product("hqk,khe->qhe", scores_grad, keys)
    keys_grad = product("hqk,qhe->khe", scores_grad, queries)
    projected_grad = jnp.concatenate(
        [grad.reshape(tokens, -1).astype(BF16) for grad in (queries_grad, keys_grad, values_grad)],
        axis=1,
    )
    normed_part = dot(projected_grad, projections, NT)
    normed_part, sources = lax.optimization_barrier(
        (normed_part, (self_rows, projected_grad, third_rows, attended))
    )
    normed_self_grad = summed_rows(normed_part)
    attention_grads = jnp.concatenate(
        [dot(sources[1], sources[0], TN).T, dot(sources[3], sources[2], TN).T], axis=1
    )
    attention_grads = row_major(attention_grads.astype(BF16))
    normed_self_grad, attention_grads = lax.optimization_barrier(
        (normed_self_grad, attention_grads)
    )
    attention_grads = summed_over_images(attention_grads).astype(F32)
    query_grad, key_grad, value_grad, output_grad = jnp.split(attention_grads, 4, axis=1)

    second_input_grad, selfnorm_grad = norm_backward(
        self_hat, self_norm_scale, selfnorm, normed_self_grad
    )
    second_grad = third_grad + second_input_grad
    first_grad, crossnorm_grad, cross_pair = mlp_backward(
        second_grad, crossnorm, cross_up, cross_down, cross_stored
    )
    first_low = first_grad.astype(BF16)
    slope_map = dot(value_map, first_low, NT).astype(BF16)
    offset = -jnp.sum(slope_map.astype(F32) * mixed, axis=0, keepdims=True)
    offset_high = offset.astype(BF16)
    offset_low = (offset - offset_high.astype(F32)).astype(BF16)
    slope_map = jnp.where(row_index == channels, offset_high, slope_map)
    slope_map = jnp.where(row_index == channels + 2, offset_low, slope_map)
    slope_map, cross_pair = lax.optimization_barrier((slope_map, cross_pair))
    slope_maps = jnp.concatenate(gathered(slope_map), axis=1)
    slope_maps, cross_pair, self_pair = lax.optimization_barrier(
        (slope_maps, pair_gradients(cross_pair), self_pair)
    )
    cross_pair = summed_over_images(cross_pair)
    selfup_grad, selfdown_grad = scattered_pair(self_pair)
    inputs_grad, partial_z, partial_gain = cross_backward(
        extent, raw, x, probs, factor, score_maps, slope_maps, gain_column
    )

    partial_z, partial_gain, selfup_grad, selfdown_grad = lax.optimization_barrier(
        (partial_z, partial_gain, selfup_grad, selfdown_grad)
    )
    value_sum = dot(mixed_low, first_low, NN)
    key_sum = dot((partial_z * cross_scale).astype(BF16), hat_rows, NN)
    inputgain_part = jnp.sum(partial_gain, axis=1)
    value_sum = jnp.where(row_index == channels, crossnorm_grad[None], value_sum)
    value_sum = jnp.where(row_index == channels + 1, selfnorm_grad[None], value_sum)
    value_sum = jnp.where(row_index == channels + 2, mlpnorm_grad[None], value_sum)
    wide_gain = jnp.pad(inputgain_part, (0, width - rows))
    key_sum = jnp.where(row_index == channels, wide_gain[None], key_sum)
    shared, partial_z, cross_pair = reduced_everywhere(
        jnp.concatenate([value_sum, key_sum], axis=0), partial_z, cross_pair
    )
    crossup_grad, crossdown_grad = scattered_pair(cross_pair)
    value_sum, key_sum = shared[:rows], shared[rows:]

    z_blocks = jnp.split(partial_z, group, axis=1)
    z_parts = exchanged([z_blocks[0]] + [part.astype(BF16) for part in z_blocks[1:]])
    z_own = (sum(part.astype(F32) for part in z_parts) * cross_scale).astype(BF16)
    latent_normed_grad = dot(z_own, key_map, TN)
    latent_input_grad, _ = norm_backward(latent_hat, latent_scale, latentgain, latent_normed_grad)
    latents_grad = first_grad + latent_input_grad

    inputgain_grad = key_sum[channels, :channels].astype(F32)
    crossnorm_grad = value_sum[channels].astype(F32)
    selfnorm_grad = value_sum[channels + 1].astype(F32)
    mlpnorm_grad = value_sum[channels + 2].astype(F32)
    value_sum, key_sum = value_sum[:channels], key_sum[:channels]
    latentgain_grad = jnp.sum(
        key_map[:channels].astype(F32) * key_sum.astype(F32), axis=0
    )
    key_scaled = (key_sum.astype(F32) * latentgain).astype(BF16)
    crossquery_grad = row_major(dot(key_scaled, crosskey, TN))
    crosskey_grad = dot(key_scaled, crossquery, NN)
    crossoutput_grad = row_major(dot(crossvalue, value_sum, TN))
    crossvalue_grad = dot(value_sum, crossoutput, NT)

    return (
        latents_out[None],
        latents_grad[None],
        jnp.transpose(inputs_grad, (1, 2, 0)),
        latentgain_grad,
        inputgain_grad,
        crossquery_grad,
        crosskey_grad,
        crossvalue_grad,
        crossoutput_grad,
        crossnorm_grad,
        crossup_grad,
        crossdown_grad,
        selfnorm_grad,
        query_grad,
        key_grad,
        value_grad,
        output_grad.T,
        mlpnorm_grad,
        selfup_grad,
        selfdown_grad,
    )


def solution(mesh):
    rows = P("dp", "mp", None)
    columns = P(None, "mp")
    outer = P("mp", None)
    whole = P()
    split = P("dp", "mp")
    turned = P("mp", "dp")
    return jax.shard_map(
        shards,
        mesh=mesh,
        in_specs=(
            rows,
            rows,
            P("dp"),
            whole,
            whole,
            whole,
            whole,
            whole,
            whole,
            whole,
            columns,
            outer,
            whole,
            columns,
            columns,
            columns,
            outer,
            whole,
            columns,
            outer,
            rows,
        ),
        out_specs=(
            rows,
            rows,
            rows,
            whole,
            whole,
            whole,
            whole,
            whole,
            whole,
            whole,
            split,
            turned,
            whole,
            split,
            split,
            split,
            turned,
            whole,
            split,
            turned,
        ),
        check_vma=False,
    )
```

```python
import functools

import jax
import jax.numpy as jnp
from jax import lax
from jax.experimental.layout import Layout, with_layout_constraint
from jax.experimental import pallas as pl
from jax.experimental.pallas import tpu as pltpu
from jax.sharding import PartitionSpec as P

HEADS = 8
EPSILON = 1e-05
MASKED = -1e30
FLOOR = -1e25
TILE = 1152
VMEM_LIMIT = 60 * 1024 * 1024
BF16 = jnp.bfloat16
F32 = jnp.float32
NN = (((1,), (0,)), ((), ()))
NT = (((1,), (1,)), ((), ()))
TN = (((0,), (0,)), ((), ()))


def dot(left, right, dims):
    return lax.dot_general(left, right, dims, preferred_element_type=F32)


def padded_rows(channels):
    return -(-(channels + 3) // 16) * 16


def normalized(raw_ref, channels, head_rows):
    top = raw_ref[:head_rows, :].astype(F32)
    rest = raw_ref[head_rows:, :].astype(F32)
    keep = lax.broadcasted_iota(jnp.int32, rest.shape, 0) < (channels - head_rows)
    rest = jnp.where(keep, rest, 0.0)
    mean = (jnp.sum(top, 0, keepdims=True) + jnp.sum(rest, 0, keepdims=True)) * (1.0 / channels)
    top = top - mean
    rest = jnp.where(keep, rest - mean, 0.0)
    square = jnp.sum(top * top, 0, keepdims=True) + jnp.sum(rest * rest, 0, keepdims=True)
    scale = lax.rsqrt(square * (1.0 / channels) + EPSILON)
    return top * scale, rest * scale, scale, keep


def prepare_kernel(limit_ref, raw_ref, gain_ref, out_ref, *, channels, head_rows):
    top, rest, _, keep = normalized(raw_ref, channels, head_rows)
    out_ref[:head_rows, :] = (top * gain_ref[:head_rows, :]).astype(BF16)
    lane = pl.program_id(0) * TILE + lax.broadcasted_iota(jnp.int32, rest.shape, 1)
    row = lax.broadcasted_iota(jnp.int32, rest.shape, 0) + head_rows
    invalid = jnp.where(lane < limit_ref[0], 0.0, 1.0)
    ones = (row == channels) | (row == channels + 2)
    extra = jnp.where(row == channels + 1, invalid, jnp.where(ones, 1.0, 0.0))
    out_ref[head_rows:, :] = jnp.where(keep, rest * gain_ref[head_rows:, :], extra).astype(BF16)


def prepare(limit, raw, gain_column):
    channels, count = raw.shape
    rows = padded_rows(channels)
    tiles = pl.cdiv(count, TILE)
    return pl.pallas_call(
        functools.partial(prepare_kernel, channels=channels, head_rows=rows - 16),
        grid_spec=pltpu.PrefetchScalarGridSpec(
            num_scalar_prefetch=1,
            grid=(tiles,),
            in_specs=[
                pl.BlockSpec((rows, TILE), lambda i, _: (0, i)),
                pl.BlockSpec((rows, 1), lambda i, _: (0, 0)),
            ],
            out_specs=pl.BlockSpec((rows, TILE), lambda i, _: (0, i)),
        ),
        out_shape=jax.ShapeDtypeStruct((rows, tiles * TILE), BF16),
        compiler_params=pltpu.CompilerParams(vmem_limit_bytes=VMEM_LIMIT),
        name="prepare",
    )(limit, raw, gain_column)


def forward_kernel(x_ref, a_ref, p_ref, y_ref, top_ref, running):
    @pl.when(pl.program_id(0) == 0)
    def _():
        running[...] = jnp.full_like(running, FLOOR)
        y_ref[...] = jnp.zeros_like(y_ref)

    x = x_ref[...]
    scores = dot(x, a_ref[...], TN)
    old = running[0:1, :]
    new = jnp.maximum(old, jnp.max(scores, 0, keepdims=True))
    probs = jnp.exp(scores - new).astype(BF16)
    p_ref[...] = probs
    y_ref[...] = y_ref[...] * jnp.exp(old - new) + dot(x, probs, NN)
    running[0:1, :] = new
    top_ref[0] = new


def cross_forward(x, a):
    rows, count = x.shape
    queries = a.shape[1]
    tiles = count // TILE
    return pl.pallas_call(
        forward_kernel,
        grid=(tiles,),
        in_specs=[
            pl.BlockSpec((rows, TILE), lambda i: (0, i)),
            pl.BlockSpec((rows, queries), lambda i: (0, 0)),
        ],
        out_specs=[
            pl.BlockSpec((TILE, queries), lambda i: (i, 0)),
            pl.BlockSpec((rows, queries), lambda i: (0, 0)),
            pl.BlockSpec((1, 1, queries), lambda i: (i, 0, 0)),
        ],
        out_shape=[
            jax.ShapeDtypeStruct((count, queries), BF16),
            jax.ShapeDtypeStruct((rows, queries), F32),
            jax.ShapeDtypeStruct((tiles, 1, queries), F32),
        ],
        scratch_shapes=[pltpu.VMEM((8, queries), F32)],
        compiler_params=pltpu.CompilerParams(vmem_limit_bytes=VMEM_LIMIT),
        name="cross_forward",
    )(x, a)


def lane_sums(values):
    total = values[:, :128]
    for k in range(1, values.shape[1] // 128):
        total = total + values[:, 128 * k : 128 * (k + 1)]
    return total


def backward_kernel(
    limit_ref,
    raw_ref,
    x_ref,
    p_ref,
    factor_ref,
    a_ref,
    b_ref,
    gain_ref,
    out_ref,
    z_ref,
    gain_grad_ref,
    *,
    channels,
    head_rows,
    guard,
):
    @pl.when(pl.program_id(0) == 0)
    def _():
        z_ref[...] = jnp.zeros_like(z_ref)
        gain_grad_ref[...] = jnp.zeros_like(gain_grad_ref)

    x = x_ref[...]
    slope = dot(x, b_ref[...], TN)
    probs = p_ref[...].astype(F32) * factor_ref[0]
    score_grad = (probs * slope).astype(BF16)
    probs = probs.astype(BF16)
    z_ref[...] += dot(x, score_grad, NN)
    grad = dot(a_ref[...], score_grad, NT) + dot(b_ref[...], probs, NT)
    top, rest, scale, keep = normalized(raw_ref, channels, head_rows)
    grad_top = grad[:head_rows]
    grad_rest = jnp.where(keep, grad[head_rows:], 0.0)
    if guard:
        lane = pl.program_id(0) * TILE + lax.broadcasted_iota(jnp.int32, (1, TILE), 1)
        inside = lane < limit_ref[0]
        grad_top = jnp.where(inside, grad_top, 0.0)
        grad_rest = jnp.where(inside, grad_rest, 0.0)
        top = jnp.where(inside, top, 0.0)
        rest = jnp.where(inside, rest, 0.0)
        scale = jnp.where(inside, scale, 0.0)
    gain_grad_ref[:head_rows, :] += lane_sums(grad_top * top)
    gain_grad_ref[head_rows:, :] += lane_sums(grad_rest * rest)
    grad_top = grad_top * gain_ref[:head_rows, :]
    grad_rest = grad_rest * gain_ref[head_rows:, :]
    mean = jnp.sum(grad_top, 0, keepdims=True) + jnp.sum(grad_rest, 0, keepdims=True)
    along = jnp.sum(grad_top * top, 0, keepdims=True) + jnp.sum(grad_rest * rest, 0, keepdims=True)
    mean = mean * (1.0 / channels)
    along = along * (1.0 / channels)
    out_ref[:head_rows, 0, :] = (grad_top - mean - top * along) * scale
    out_rest = (grad_rest - mean - rest * along) * scale
    out_ref[head_rows:, 0, :] = out_rest[: channels - head_rows]


def cross_backward(limit, raw, x, probs, factor, a, b, gain_column):
    channels, real = raw.shape
    rows, count = x.shape
    queries = a.shape[1]
    tiles = count // TILE
    return pl.pallas_call(
        functools.partial(
            backward_kernel, channels=channels, head_rows=rows - 16, guard=count != real
        ),
        grid_spec=pltpu.PrefetchScalarGridSpec(
            num_scalar_prefetch=1,
            grid=(tiles,),
            in_specs=[
                pl.BlockSpec((rows, TILE), lambda i, _: (0, i)),
                pl.BlockSpec((rows, TILE), lambda i, _: (0, i)),
                pl.BlockSpec((TILE, queries), lambda i, _: (i, 0)),
                pl.BlockSpec((1, 1, queries), lambda i, _: (i, 0, 0)),
                pl.BlockSpec((rows, queries), lambda i, _: (0, 0)),
                pl.BlockSpec((rows, queries), lambda i, _: (0, 0)),
                pl.BlockSpec((rows, 1), lambda i, _: (0, 0)),
            ],
            out_specs=[
                pl.BlockSpec((channels, 1, TILE), lambda i, _: (0, 0, i)),
                pl.BlockSpec((rows, queries), lambda i, _: (0, 0)),
                pl.BlockSpec((rows, 128), lambda i, _: (0, 0)),
            ],
        ),
        out_shape=[
            jax.ShapeDtypeStruct((channels, 1, real), F32),
            jax.ShapeDtypeStruct((rows, queries), F32),
            jax.ShapeDtypeStruct((rows, 128), F32),
        ],
        compiler_params=pltpu.CompilerParams(vmem_limit_bytes=VMEM_LIMIT),
        name="cross_backward",
    )(limit, raw, x, probs, factor, a, b, gain_column)


def shifted(block, distance):
    size = lax.axis_size("mp")
    return lax.ppermute(block, "mp", [(i, (i + distance) % size) for i in range(size)])


def gathered(block):
    size = lax.axis_size("mp")
    return [block] + [shifted(block, d) for d in range(1, size)]


def exchanged(blocks):
    return [blocks[0]] + [shifted(blocks[d], -d) for d in range(1, len(blocks))]


def summed_rows(partial):
    size = lax.axis_size("mp")
    blocks = jnp.split(partial, size, axis=0)
    sent = [blocks[0]] + [block.astype(BF16) for block in blocks[1:]]
    total = sent[0]
    for block in exchanged(sent)[1:]:
        total = total + block.astype(F32)
    return total


def reduced_everywhere(values, held, later):
    data, size = lax.axis_size("dp"), lax.axis_size("mp")
    index = lax.axis_index("dp")
    bits = [1 << k for k in range(data.bit_length() - 1)]
    for bit in bits:
        low, high = jnp.split(values, 2, axis=1)
        upper = (index & bit) != 0
        mine = jnp.where(upper, high, low)
        other = jnp.where(upper, low, high).astype(BF16)
        swap = [(i, i ^ bit) for i in range(data)]
        values = mine + lax.ppermute(other, "dp", swap).astype(F32)
        if bit == bits[0]:
            values, held = lax.optimization_barrier((values, held))
    rows, columns = values.shape
    chunks = values.reshape(size, rows // size, columns)
    place = lax.axis_index("mp")

    def chunk(k):
        return lax.dynamic_index_in_dim(chunks, (place + k) % size, 0, keepdims=False)

    total = chunk(0)
    for d in range(1, size):
        total = total + shifted(chunk(d).astype(BF16), d).astype(F32)
    own = total.astype(BF16)
    full = jnp.zeros((size,) + own.shape, BF16)
    for d, block in enumerate(gathered(own)):
        full = lax.dynamic_update_index_in_dim(full, block, (place - d) % size, 0)
    full = full.reshape(rows, columns)
    full, later = lax.optimization_barrier((full, later))
    for bit in reversed(bits):
        swap = [(i, i ^ bit) for i in range(data)]
        other = lax.ppermute(full, "dp", swap)
        upper = (index & bit) != 0
        full = jnp.where(
            upper, jnp.concatenate([other, full], 1), jnp.concatenate([full, other], 1)
        )
    return full, held, later


def standardized(values):
    centred = values - jnp.mean(values, axis=-1, keepdims=True)
    spread = jnp.mean(centred * centred, axis=-1, keepdims=True)
    scale = lax.rsqrt(spread + EPSILON)
    return centred * scale, scale


def norm_backward(hat, scale, gain, upstream):
    weighted = upstream * gain
    mean = jnp.mean(weighted, axis=-1, keepdims=True)
    along = jnp.mean(weighted * hat, axis=-1, keepdims=True)
    return (weighted - mean - hat * along) * scale, jnp.sum(upstream * hat, axis=0)


def gelu_tanh(values):
    return jax.nn.gelu(values, approximate=True)


def gelu_backward(values, upstream):
    return jax.vjp(gelu_tanh, values)[1](upstream)[0]


def whole_weights(up, down):
    data = lax.axis_size("dp")
    index = lax.axis_index("dp")
    pair = jnp.stack([up.T, down])
    part = pair.shape[1] // data
    piece = lax.dynamic_slice_in_dim(pair, index * part, part, 1)
    full = lax.all_gather(piece, ("mp", "dp"), axis=1, tiled=True)
    return full[0], full[1]


def mlp_forward(residual, gain, up, down):
    hat, scale = standardized(residual)
    normed = (hat * gain).astype(BF16)
    hidden = dot(normed, up, NT)
    active = gelu_tanh(hidden).astype(BF16)
    return residual + dot(active, down, NN), (hat, scale, normed, hidden, active)


def mlp_backward(upstream, gain, up, down, stored):
    hat, scale, normed, hidden, active = stored
    low = upstream.astype(BF16)
    active_grad = dot(low, down, NT)
    hidden_grad = gelu_backward(hidden, active_grad).astype(BF16)
    normed_grad = dot(hidden_grad, up, NN)
    input_grad, gain_grad = norm_backward(hat, scale, gain, normed_grad)
    return upstream + input_grad, gain_grad, (normed, hidden_grad, low, active)


def pair_gradients(operands):
    normed, hidden_grad, low, active = operands
    size = lax.axis_size("mp")
    grads = (dot(hidden_grad, normed, TN).T, dot(active, low, TN).T)
    pieces = [jnp.split(grad.astype(BF16), size, axis=1) for grad in grads]
    return row_major(jnp.concatenate([piece[k] for k in range(size) for piece in pieces], axis=1))


def row_major(values):
    return with_layout_constraint(values, Layout((0, 1)))


def summed_over_images(stacked):
    return lax.psum_scatter(stacked, "dp", scatter_dimension=0, tiled=True)


def scattered_pair(mine, after=()):
    size = lax.axis_size("mp")
    part = mine.shape[1] // size
    place = lax.axis_index("mp")

    def chunk(k):
        return lax.dynamic_slice_in_dim(mine, (place + k) % size * part, part, 1)

    blocks = [chunk(0)] + [shifted(chunk(d), d) for d in range(1, size)]
    blocks, after = lax.optimization_barrier((blocks, after))
    total = sum(block.astype(F32) for block in blocks)
    first, second = jnp.split(total, 2, axis=1)
    return first, second.T, after


def shards(
    latents,
    inputs,
    image_sizes,
    latentgain,
    inputgain,
    crossquery,
    crosskey,
    crossvalue,
    crossoutput,
    crossnorm,
    crossup,
    crossdown,
    selfnorm,
    selfquery,
    selfkey,
    selfvalue,
    selfoutput,
    mlpnorm,
    selfup,
    selfdown,
    cotangent,
):
    width = latents.shape[-1]
    channels = inputs.shape[-1]
    count = inputs.shape[1]
    head_size = width // HEADS
    rows = padded_rows(channels)
    group = lax.axis_size("mp")
    cross_scale = width**-0.5
    self_scale = head_size**-0.5

    cross_up, cross_down = whole_weights(crossup, crossdown)
    self_up, self_down = whole_weights(selfup, selfdown)

    latent_float = latents[0].astype(F32)
    padding = ((0, rows - channels), (0, 0))
    key_weight = jnp.pad(crosskey, padding)
    value_weight = jnp.pad(crossvalue, padding)
    key_map = dot(key_weight, crossquery, NT).astype(BF16)

    latent_hat, latent_scale = standardized(latent_float)
    normed_latent = (latent_hat * latentgain).astype(BF16)
    row_index = lax.broadcasted_iota(jnp.int32, (rows, 1), 0)
    score_map = dot(key_map, normed_latent, NT) * cross_scale
    score_map = jnp.where(row_index == channels + 1, MASKED, score_map).astype(BF16)
    score_maps = jnp.concatenate(gathered(score_map), axis=1)
    hat_rows = jnp.concatenate(gathered(latent_hat.astype(BF16)), axis=0)

    limit = jnp.clip(image_sizes - lax.axis_index("mp") * count, 0, count)
    extent = jnp.full((1,), count, jnp.int32)
    raw = inputs[0].T
    gain_column = jnp.pad(inputgain[:, None], padding)
    x = prepare(limit, raw, gain_column)
    probs, partial, tops = cross_forward(x, score_maps)

    partial = jnp.where(row_index == channels + 1, tops[-1], partial)
    partial, value_weight = lax.optimization_barrier((partial, value_weight))
    value_map = dot(value_weight, crossoutput, NN).astype(BF16)
    parts = exchanged(jnp.split(partial, group, axis=1))
    part_tops = [part[channels + 1 : channels + 2] for part in parts]
    top = functools.reduce(jnp.maximum, part_tops)
    mixed = sum(part * jnp.exp(part_top - top) for part, part_top in zip(parts, part_tops))
    total = mixed[channels : channels + 1]
    log_total = top + jnp.log(total)
    mixed = jnp.where(row_index < channels, mixed / total, 0.0)
    log_all = jnp.concatenate(gathered(log_total), axis=1)
    mixed_low = mixed.astype(BF16)

    first_resid = latent_float + dot(mixed_low, value_map, TN)
    second_resid, cross_stored = mlp_forward(first_resid, crossnorm, cross_up, cross_down)

    self_hat, self_norm_scale = standardized(second_resid)
    normed_self = (self_hat * selfnorm).astype(BF16)
    normed_self, log_all = lax.optimization_barrier((normed_self, log_all))
    factor = jnp.exp(tops - log_all[None])
    self_rows = jnp.concatenate(gathered(normed_self), axis=0)
    tokens = self_rows.shape[0]
    projections = jnp.concatenate([selfquery, selfkey, selfvalue], axis=1)
    block = selfquery.shape[1]
    projected = dot(self_rows, projections, NN).astype(BF16)

    def heads_of(flat):
        return flat.reshape(tokens, -1, head_size)

    queries, keys, values = (
        heads_of(projected[:, k * block : (k + 1) * block]) for k in range(3)
    )

    def product(pattern, left, right):
        return jnp.einsum(pattern, left, right, preferred_element_type=F32)

    scores = product("qhe,khe->hqk", queries, keys) * self_scale
    self_top = jnp.max(scores, axis=-1, keepdims=True)
    powers = jnp.exp(scores - self_top)
    self_probs = powers / jnp.sum(powers, axis=-1, keepdims=True)
    self_low = self_probs.astype(BF16)
    attended = product("hqk,khe->qhe", self_low, values).reshape(tokens, -1).astype(BF16)
    third_resid = second_resid + summed_rows(dot(attended, selfoutput, NN))
    final_resid, self_stored = mlp_forward(third_resid, mlpnorm, self_up, self_down)
    latents_out = final_resid.astype(BF16)

    upstream = cotangent[0].astype(F32)
    third_grad, mlpnorm_grad, self_pair = mlp_backward(
        upstream, mlpnorm, self_up, self_down, self_stored
    )
    third_low, self_pair = lax.optimization_barrier((third_grad.astype(BF16), self_pair))
    third_rows = jnp.concatenate(gathered(third_low), axis=0)
    third_rows, self_pair = lax.optimization_barrier((third_rows, pair_gradients(self_pair)))
    self_pair = summed_over_images(self_pair)
    attended_grad = heads_of(dot(third_rows, selfoutput, NT).astype(BF16))
    self_probs_grad = product("qhe,khe->hqk", attended_grad, values)
    self_row = jnp.sum(self_probs * self_probs_grad, axis=-1, keepdims=True)
    scores_grad = (self_probs * (self_probs_grad - self_row) * self_scale).astype(BF16)
    scores_grad = lax.optimization_barrier(scores_grad)
    values_grad = product("hqk,qhe->khe", self_low, attended_grad)
    queries_grad = product("hqk,khe->qhe", scores_grad, keys)
    keys_grad = product("hqk,qhe->khe", scores_grad, queries)
    projected_grad = jnp.concatenate(
        [grad.reshape(tokens, -1).astype(BF16) for grad in (queries_grad, keys_grad, values_grad)],
        axis=1,
    )
    normed_part = dot(projected_grad, projections, NT)
    normed_part, sources = lax.optimization_barrier(
        (normed_part, (self_rows, projected_grad, third_rows, attended))
    )
    normed_self_grad = summed_rows(normed_part)
    attention_grads = jnp.concatenate(
        [dot(sources[1], sources[0], TN).T, dot(sources[3], sources[2], TN).T], axis=1
    )
    attention_grads = row_major(attention_grads.astype(BF16))
    normed_self_grad, attention_grads = lax.optimization_barrier(
        (normed_self_grad, attention_grads)
    )
    attention_grads = summed_over_images(attention_grads).astype(F32)
    query_grad, key_grad, value_grad, output_grad = jnp.split(attention_grads, 4, axis=1)

    second_input_grad, selfnorm_grad = norm_backward(
        self_hat, self_norm_scale, selfnorm, normed_self_grad
    )
    second_grad = third_grad + second_input_grad
    first_grad, crossnorm_grad, cross_pair = mlp_backward(
        second_grad, crossnorm, cross_up, cross_down, cross_stored
    )
    first_low = first_grad.astype(BF16)
    slope_map = dot(value_map, first_low, NT).astype(BF16)
    offset = -jnp.sum(slope_map.astype(F32) * mixed, axis=0, keepdims=True)
    offset_high = offset.astype(BF16)
    offset_low = (offset - offset_high.astype(F32)).astype(BF16)
    slope_map = jnp.where(row_index == channels, offset_high, slope_map)
    slope_map = jnp.where(row_index == channels + 2, offset_low, slope_map)
    slope_map, cross_pair = lax.optimization_barrier((slope_map, cross_pair))
    slope_maps = jnp.concatenate(gathered(slope_map), axis=1)
    slope_maps, cross_pair, self_pair = lax.optimization_barrier(
        (slope_maps, pair_gradients(cross_pair), self_pair)
    )
    cross_pair = summed_over_images(cross_pair)
    selfup_grad, selfdown_grad, _ = scattered_pair(self_pair)
    inputs_grad, partial_z, partial_gain = cross_backward(
        extent, raw, x, probs, factor, score_maps, slope_maps, gain_column
    )

    partial_z, partial_gain, selfup_grad, selfdown_grad = lax.optimization_barrier(
        (partial_z, partial_gain, selfup_grad, selfdown_grad)
    )
    value_sum = dot(mixed_low, first_low, NN)
    key_sum = dot((partial_z * cross_scale).astype(BF16), hat_rows, NN)
    inputgain_part = jnp.sum(partial_gain, axis=1)
    value_sum = jnp.where(row_index == channels, crossnorm_grad[None], value_sum)
    value_sum = jnp.where(row_index == channels + 1, selfnorm_grad[None], value_sum)
    value_sum = jnp.where(row_index == channels + 2, mlpnorm_grad[None], value_sum)
    wide_gain = jnp.pad(inputgain_part, (0, width - rows))
    key_sum = jnp.where(row_index == channels, wide_gain[None], key_sum)
    shared, partial_z, cross_pair = reduced_everywhere(
        jnp.concatenate([value_sum, key_sum], axis=0), partial_z, cross_pair
    )
    value_sum, key_sum = shared[:rows], shared[rows:]

    z_blocks = jnp.split(partial_z, group, axis=1)
    z_parts = exchanged([z_blocks[0]] + [part.astype(BF16) for part in z_blocks[1:]])
    z_own = (sum(part.astype(F32) for part in z_parts) * cross_scale).astype(BF16)
    latent_normed_grad = dot(z_own, key_map, TN)
    latent_input_grad, _ = norm_backward(latent_hat, latent_scale, latentgain, latent_normed_grad)
    latents_grad = first_grad + latent_input_grad

    inputgain_grad = key_sum[channels, :channels].astype(F32)
    crossnorm_grad = value_sum[channels].astype(F32)
    selfnorm_grad = value_sum[channels + 1].astype(F32)
    mlpnorm_grad = value_sum[channels + 2].astype(F32)
    value_sum, key_sum = value_sum[:channels], key_sum[:channels]
    latentgain_grad = jnp.sum(
        key_map[:channels].astype(F32) * key_sum.astype(F32), axis=0
    )
    key_scaled = (key_sum.astype(F32) * latentgain).astype(BF16)
    crossquery_grad = row_major(dot(key_scaled, crosskey, TN))
    crosskey_grad = dot(key_scaled, crossquery, NN)
    crossoutput_grad = row_major(dot(crossvalue, value_sum, TN))
    crossvalue_grad = dot(value_sum, crossoutput, NT)
    finals = (crossquery_grad, crosskey_grad, crossoutput_grad, crossvalue_grad)
    crossup_grad, crossdown_grad, finals = scattered_pair(cross_pair, finals)
    crossquery_grad, crosskey_grad, crossoutput_grad, crossvalue_grad = finals

    return (
        latents_out[None],
        latents_grad[None],
        jnp.transpose(inputs_grad, (1, 2, 0)),
        latentgain_grad,
        inputgain_grad,
        crossquery_grad,
        crosskey_grad,
        crossvalue_grad,
        crossoutput_grad,
        crossnorm_grad,
        crossup_grad,
        crossdown_grad,
        selfnorm_grad,
        query_grad,
        key_grad,
        value_grad,
        output_grad.T,
        mlpnorm_grad,
        selfup_grad,
        selfdown_grad,
    )


def solution(mesh):
    rows = P("dp", "mp", None)
    columns = P(None, "mp")
    outer = P("mp", None)
    whole = P()
    split = P("dp", "mp")
    turned = P("mp", "dp")
    return jax.shard_map(
        shards,
        mesh=mesh,
        in_specs=(
            rows,
            rows,
            P("dp"),
            whole,
            whole,
            whole,
            whole,
            whole,
            whole,
            whole,
            columns,
            outer,
            whole,
            columns,
            columns,
            columns,
            outer,
            whole,
            columns,
            outer,
            rows,
        ),
        out_specs=(
            rows,
            rows,
            rows,
            whole,
            whole,
            whole,
            whole,
            whole,
            whole,
            whole,
            split,
            turned,
            whole,
            split,
            split,
            split,
            turned,
            whole,
            split,
            turned,
        ),
        check_vma=False,
    )
```
